512 devices in a mesh: gx: 16 (over y, core), gy: 8 (over z), layer: 4 (over x).
Axes of the slice: x: 4, y: 8, z: 8, core: 2. Of those that a mesh axis runs over, the one named last changes fastest.
Arguments:
- source: float32 [3, 32, 128, 2048], P(None, 'layer', 'gy', 'gx'), may hold values from -6 to 6
- active_cells: int32 [32, 128, 2048], P('layer', 'gy', 'gx'), may hold values 0 or 1
- diag_blocks: float32 [9, 32, 128, 2048], P(None, 'layer', 'gy', 'gx'), may hold values from -0.45 to 3, as said below
- frozen_inverses: float32 [9, 32, 128, 2048], P(None, 'layer', 'gy', 'gx'), may hold values from -0.05 to 0.2, as said below
- transmissibility: float32 [3, 32, 128, 2048], P(None, 'layer', 'gy', 'gx'), may hold values from 0.1 to 1
- pressure_weights: float32 [3, 32, 128, 2048], P(None, 'layer', 'gy', 'gx'), may hold values from 1 to 4
- stencil_fine: float32 [7, 32, 128, 2048], P(None, 'layer', 'gy', 'gx'), may hold values from -1 to 9, as said below
- coarse_one: float32 [7, 16, 64, 1024], P(None, 'layer', 'gy', 'gx'), may hold values from -1 to 9, as said below
- coarse_two: float32 [7, 8, 32, 512], P(None, 'layer', 'gy', 'gx'), may hold values from -1 to 9, as said below
- coarse_three: float32 [7, 4, 16, 256], P(None, 'layer', 'gy', 'gx'), may hold values from -1 to 9, as said below
- pressure_state: float32 [32, 128, 2048], P('layer', 'gy', 'gx'), may hold values from -6 to 6
- mobilities: float32 [3, 32, 128, 2048], P(None, 'layer', 'gy', 'gx'), may hold values from 0.1 to 1
Outputs:
- adjoint: float32 [3, 32, 128, 2048], P(None, 'layer', 'gy', 'gx')
- perm_grad: float32 [3, 32, 128, 2048], P(None, 'layer', 'gy', 'gx')
The draws below stay inside these ranges and needn't reach their ends.
Inputs may be any that keep to these rules, and one draw needn't show every extreme that they name: `diag_blocks`: entries 0, 4 and 8 are the blocks' diagonals. `frozen_inverses`: entries 0, 4 and 8 are the blocks' diagonals. `stencil_fine`: coefficient 0 exceeds the sum of the magnitudes of the other six. `coarse_one`: coefficient 0 exceeds the sum of the magnitudes of the other six. `coarse_two`: coefficient 0 exceeds the sum of the magnitudes of the other six. `coarse_three`: coefficient 0 exceeds the sum of the magnitudes of the other six.
All inputs are finite; a program needn't handle non-finite values. No bound on the sum of `active_cells` on one device may be relied on, other than what follows from the above.
Results may differ from the reference program's by a relative error of at most 0.00002.
Values sent between devices are 32-bit elements; how exact they have to be, the bound alone decides.
A program may use at most 64 MiB of HBM per device.

```python
import math
import jax
import jax.numpy as jnp

SWEEPS = 3
LEVELS = 3
COARSE_SWEEPS = 4
NX = 2048
NY = 128
NZ = 32


def block_draw(key, diag_low, diag_span, coupling_most, coupling_scale):
    extent = (9, NZ, NY, NX)
    first, second = jax.random.split(jax.random.fold_in(key, 11))
    on_diag = (jnp.arange(9) % 4 == 0).reshape(9, 1, 1, 1)
    diagonal = diag_low + diag_span * jax.random.uniform(first, extent, jnp.float32)
    coupling = jnp.clip(coupling_scale * jax.random.normal(second, extent, jnp.float32), -coupling_most, coupling_most)
    return jnp.where(on_diag, diagonal, coupling)


def draw_diag_blocks(key, part):
    return block_draw(key, 1.0, 2.0, 0.45, 0.15)


def draw_frozen_inverses(key, part):
    return block_draw(key, 0.1, 0.1, 0.05, 0.02)


def stencil_draw(key, extent):
    first, second = jax.random.split(jax.random.fold_in(key, 23))
    center_draw = jax.random.uniform(first, (1,) + extent, jnp.float32)
    coupling_draw = jax.random.uniform(second, (6,) + extent, jnp.float32)
    center = 6.5 + 2.5 * center_draw
    coupling = -(0.2 + 0.8 * coupling_draw)
    return jnp.concatenate([center, coupling])


def draw_stencil_fine(key, part):
    return stencil_draw(key, (NZ, NY, NX))


def draw_coarse_one(key, part):
    return stencil_draw(key, (NZ // 2, NY // 2, NX // 2))


def draw_coarse_two(key, part):
    return stencil_draw(key, (NZ // 4, NY // 4, NX // 4))


def draw_coarse_three(key, part):
    return stencil_draw(key, (NZ // 8, NY // 8, NX // 8))


def plant(drawn, stream_key, smallest, largest):
    dims = drawn.shape
    place = [jax.random.randint(jax.random.fold_in(stream_key, axis), (), 0, dims[axis]) for axis in range(len(dims))]
    drawn = drawn.at[tuple(place)].set(smallest)
    longest = dims.index(max(dims))
    place[longest] = (place[longest] + 1) % dims[longest]
    return drawn.at[tuple(place)].set(largest)


def levels(rng, shape, cuts, smallest, high):
    level, own = 1.0, jax.random.fold_in(rng, 6)
    for axis_at, blocks in cuts:
        steps = jnp.exp(jax.random.uniform(jax.random.fold_in(own, axis_at), (blocks,), jnp.float32, smallest / len(cuts), high / len(cuts)))
        level = level * jnp.repeat(steps, shape[axis_at] // blocks).reshape([-1 if axis == axis_at else 1 for axis in range(len(shape))])
    return level


def bell_draw(key, shape, spread, most, cuts=(), dtype=jnp.bfloat16):
    factor_of = levels(key, shape, cuts, -0.22, 0.18) if cuts else 1.0
    drawn = jax.random.normal(key, shape, jnp.float32) * spread * factor_of
    return jnp.minimum(jnp.maximum(drawn, -most), most).astype(dtype)


def setup_inputs(seed: int = 0) -> dict:
    keys = jax.random.split(jax.random.key(seed), 13)
    return {
        "source": bell_draw(keys[0], (3, NZ, NY, NX), 1.0, 6.0, ((1, 4), (2, 8), (3, 16)), jnp.float32),
        "active_cells": plant((jax.random.randint(keys[1], (NZ, NY, NX), 0, 10) < 9).astype(jnp.int32), jax.random.fold_in(keys[1], 1), 0, 1),
        "diag_blocks": draw_diag_blocks(jax.random.fold_in(keys[12], 71), 0),
        "frozen_inverses": draw_frozen_inverses(jax.random.fold_in(keys[12], 71), 0),
        "transmissibility": jnp.clip(jnp.exp(math.log(1.0) - 2.3025851 * jax.random.uniform(keys[4], (3, NZ, NY, NX), jnp.float32) ** levels(keys[4], (3, NZ, NY, NX), ((1, 4), (2, 8), (3, 16)), -0.2, 0.2)), 0.1, 1.0),
        "pressure_weights": jnp.clip(1.0 + 3.0 * jax.random.uniform(keys[5], (3, NZ, NY, NX), jnp.float32) ** levels(keys[5], (3, NZ, NY, NX), ((1, 4), (2, 8), (3, 16)), -0.2, 0.2), 1.0, 4.0),
        "stencil_fine": draw_stencil_fine(jax.random.fold_in(keys[12], 71), 0),
        "coarse_one": draw_coarse_one(jax.random.fold_in(keys[12], 71), 0),
        "coarse_two": draw_coarse_two(jax.random.fold_in(keys[12], 71), 0),
        "coarse_three": draw_coarse_three(jax.random.fold_in(keys[12], 71), 0),
        "pressure_state": bell_draw(keys[10], (NZ, NY, NX), 1.0, 6.0, ((0, 4), (1, 8), (2, 16)), jnp.float32),
        "mobilities": jnp.clip(jnp.exp(math.log(1.0) - 2.3025851 * jax.random.uniform(keys[11], (3, NZ, NY, NX), jnp.float32) ** levels(keys[11], (3, NZ, NY, NX), ((1, 4), (2, 8), (3, 16)), -0.2, 0.2)), 0.1, 1.0),
    }


OMEGA = 0.8


def leading(field):
    return (slice(None),) * (field.ndim - 3)


def padded_zero(field):
    widths = [(0, 0)] * (field.ndim - 3) + [(1, 1)] * 3
    return jnp.pad(field, widths)


def interior(padded):
    return padded[leading(padded) + (slice(1, -1), slice(1, -1), slice(1, -1))]


def neighbour(padded, direction, lower):
    window = [slice(1, -1), slice(1, -1), slice(1, -1)]
    window[direction] = slice(0, -2) if lower else slice(2, None)
    return padded[leading(padded) + tuple(window)]


def system_row(channel, values, padded_channel, trans_pad, blocks):
    total = blocks[channel] * values[0] + blocks[3 + channel] * values[1] + blocks[6 + channel] * values[2]
    center = interior(padded_channel)
    for direction in range(3):
        here = interior(trans_pad[direction])
        before = neighbour(trans_pad[direction], direction, True)
        total = total + here * (center - neighbour(padded_channel, direction, False))
        total = total + before * (center - neighbour(padded_channel, direction, True))
    return total


def system_apply(values, padded_values, trans_pad, blocks):
    return jnp.stack([system_row(channel, values, padded_values[channel], trans_pad, blocks) for channel in range(3)])


def frozen_apply(inverses, residual):
    return jnp.stack([inverses[channel] * residual[0] + inverses[3 + channel] * residual[1] + inverses[6 + channel] * residual[2] for channel in range(3)])


def stencil_apply(field, padded_field, center, off_pad):
    total = center * field
    for direction in range(3):
        upper_coef = off_pad[2 * direction + 1]
        lower_coef = off_pad[2 * direction]
        total = total + neighbour(upper_coef, direction, True) * neighbour(padded_field, direction, True)
        total = total + neighbour(lower_coef, direction, False) * neighbour(padded_field, direction, False)
    return total


def restrict(field):
    depth, height, width = field.shape
    return field.reshape(depth // 2, 2, height // 2, 2, width // 2, 2).sum(axis=(1, 3, 5))


def prolong(field):
    return jnp.repeat(jnp.repeat(jnp.repeat(field, 2, 0), 2, 1), 2, 2)


def coarsest_solve(rhs, stencil):
    center = stencil[0]
    off_pad = padded_zero(stencil[1:])
    field = OMEGA * rhs / center
    for sweep in range(COARSE_SWEEPS - 1):
        field = field + OMEGA * (rhs - stencil_apply(field, padded_zero(field), center, off_pad)) / center
    return field


def vcycle(rhs, stencils, level):
    if level == LEVELS:
        return coarsest_solve(rhs, stencils[level])
    stencil = stencils[level]
    center = stencil[0]
    off_pad = padded_zero(stencil[1:])
    field = OMEGA * rhs / center
    residual = rhs - stencil_apply(field, padded_zero(field), center, off_pad)
    field = field + prolong(vcycle(restrict(residual), stencils, level + 1))
    field = field + OMEGA * (rhs - stencil_apply(field, padded_zero(field), center, off_pad)) / center
    return field


def face_term(coef, lam_a, lam_b, mob_a, mob_b, pres_a, pres_b):
    total = (lam_a[0] - lam_b[0]) * (0.5 * (mob_a[0] + mob_b[0]))
    for channel in (1, 2):
        total = total + (lam_a[channel] - lam_b[channel]) * (0.5 * (mob_a[channel] + mob_b[channel]))
    return coef * total * (pres_a - pres_b)


def reference(source, active_cells, diag_blocks, frozen_inverses, transmissibility, pressure_weights, stencil_fine, coarse_one, coarse_two, coarse_three, pressure_state, mobilities):
    mask = active_cells.astype(jnp.float32)
    rhs = source * mask
    trans_pad = padded_zero(transmissibility)
    iterate = frozen_apply(frozen_inverses, rhs)
    for sweep in range(SWEEPS - 1):
        iterate = iterate + frozen_apply(frozen_inverses, rhs - system_apply(iterate, padded_zero(iterate), trans_pad, diag_blocks))
    row = system_row(0, iterate, padded_zero(iterate[0]), trans_pad, diag_blocks)
    pressure_rhs = rhs[0] - row
    correction = vcycle(pressure_rhs, (stencil_fine, coarse_one, coarse_two, coarse_three), 0)
    adjoint = mask * (iterate + pressure_weights * correction[None])
    states = jnp.concatenate([adjoint, mobilities, pressure_state[None]])
    states_pad = padded_zero(states)
    gradients = []
    for direction in range(3):
        above = neighbour(states_pad, direction, False)
        here_term = face_term(transmissibility[direction], adjoint, above[0:3], mobilities, above[3:6], pressure_state, above[6])
        below_term = neighbour(padded_zero(here_term), direction, True)
        gradients.append(0.5 * (here_term + below_term))
    return adjoint, jnp.stack(gradients)
```

```python
import functools

import jax
import jax.numpy as jnp
from jax import lax
from jax.experimental import pallas as pl
from jax.experimental.pallas import tpu as pltpu
from jax.sharding import PartitionSpec as P

MESH = pl.DeviceIdType.MESH
OMEGA = 0.8
LEVELS = 3
COARSE_SWEEPS = 4
AXES = ("layer", "gy", "gx")
NZ, NY, NX = 8, 16, 128
PLANE = (NY, NX)

ROUNDS = {
    "first": (4, 3, 8),
    "second": (3, 3, 8),
    "third": (1, 1, 8),
    "saved": (4, 4, 8),
    "down0": (1, 1, 8),
    "down1": (1, 1, 4),
    "down2": (1, 1, 2),
    "base0": (1, 1, 1),
    "base1": (1, 1, 1),
    "base2": (1, 1, 1),
    "up2": (1, 1, 2),
    "up1": (1, 1, 4),
    "up0": (1, 1, 8),
    "last": (3, 3, 8),
}
ROUND_NAMES = list(ROUNDS)

INPUTS = (
    "source",
    "active",
    "blocks",
    "inverses",
    "trans",
    "weights",
    "fine",
    "one",
    "two",
    "three",
    "pressure",
    "mobilities",
)
LOAD_ORDER = (
    "source",
    "active",
    "inverses",
    "trans",
    "blocks",
    "mobilities",
    "pressure",
    "fine",
    "one",
    "two",
    "three",
    "weights",
)


def message_shape(name, dim, up):
    fields_up, fields_down, planes = ROUNDS[name]
    fields = fields_up if up else fields_down
    if dim == 0:
        return (fields, NY, NX)
    if dim == 1:
        return (fields, planes, NX)
    return PLANE


def scratch_table(shapes):
    table = {}
    for name in INPUTS:
        table["in_" + name] = pltpu.VMEM(shapes[name][0], shapes[name][1])
    field = (NZ,) + PLANE
    table["rhs"] = pltpu.VMEM((3,) + field, jnp.float32)
    table["iterate"] = pltpu.VMEM((3,) + field, jnp.float32)
    table["total"] = pltpu.VMEM((3,) + field, jnp.float32)
    table["trans_sum"] = pltpu.VMEM(field, jnp.float32)
    for level in range(LEVELS + 1):
        planes = NZ >> level
        if level:
            table[f"coef{level}"] = pltpu.VMEM((7, planes) + PLANE, jnp.float32)
        table[f"scale{level}"] = pltpu.VMEM((planes,) + PLANE, jnp.float32)
        table[f"b{level}"] = pltpu.VMEM((planes,) + PLANE, jnp.float32)
        table[f"x{level}"] = pltpu.VMEM((planes,) + PLANE, jnp.float32)
        table[f"r{level}"] = pltpu.VMEM((planes,) + PLANE, jnp.float32)
    table["face"] = pltpu.VMEM((3, 3) + field, jnp.float32)
    table["face_low_z"] = pltpu.VMEM((3,) + PLANE, jnp.float32)
    table["face_low_y"] = pltpu.VMEM((3, NZ, NX), jnp.float32)
    table["face_low_x"] = pltpu.VMEM((3,) + field, jnp.float32)
    for name in ROUNDS:
        for dim in range(3):
            for up in (0, 1):
                shape = message_shape(name, dim, up)
                table[f"send_{name}_{dim}{up}"] = pltpu.VMEM(shape, jnp.float32)
                table[f"recv_{name}_{dim}{up}"] = pltpu.VMEM(shape, jnp.float32)
    table["load_sem"] = pltpu.SemaphoreType.DMA((len(INPUTS),))
    table["send_sem"] = pltpu.SemaphoreType.DMA((6 * len(ROUNDS),))
    table["recv_sem"] = pltpu.SemaphoreType.DMA((6 * len(ROUNDS),))
    return table


def rolled(value, amount, axis):
    amount = amount % value.shape[axis]
    return pltpu.roll(value, amount, axis) if amount else value


def kernel(sizes, scratch_names, *refs):
    hbm = dict(zip(INPUTS, refs[: len(INPUTS)]))
    adjoint_ref, gradient_ref = refs[len(INPUTS) : len(INPUTS) + 2]
    ref = dict(zip(scratch_names, refs[len(INPUTS) + 2 :]))

    me = [lax.axis_index(axis) for axis in AXES]
    above = [lax.rem(me[d] + 1, sizes[d]) for d in range(3)]
    below = [lax.rem(me[d] + sizes[d] - 1, sizes[d]) for d in range(3)]

    loads = {}
    for name in LOAD_ORDER:
        loads[name] = pltpu.make_async_copy(
            hbm[name], ref["in_" + name], ref["load_sem"].at[INPUTS.index(name)]
        )
        loads[name].start()

    barrier = pltpu.get_barrier_semaphore()
    for d in range(3):
        for peer in (above[d], below[d]):
            pl.semaphore_signal(barrier, inc=1, device_id={AXES[d]: peer}, device_id_type=MESH)

    low_on = [jnp.where(me[d] > 0, 1.0, 0.0).astype(jnp.float32) for d in range(3)]
    high_on = [jnp.where(me[d] < sizes[d] - 1, 1.0, 0.0).astype(jnp.float32) for d in range(3)]

    row = lax.broadcasted_iota(jnp.int32, PLANE, 0)
    lane = lax.broadcasted_iota(jnp.int32, PLANE, 1)
    zero = jnp.zeros(PLANE, jnp.float32)
    copies = []
    arrivals = {}

    def send(name, dim):
        for up in (1, 0):
            k = ROUND_NAMES.index(name) * 6 + dim * 2 + up
            copy = pltpu.make_async_remote_copy(
                src_ref=ref[f"send_{name}_{dim}{up}"],
                dst_ref=ref[f"recv_{name}_{dim}{up}"],
                send_sem=ref["send_sem"].at[k],
                recv_sem=ref["recv_sem"].at[k],
                device_id={AXES[dim]: above[dim] if up else below[dim]},
                device_id_type=MESH,
            )
            copy.start()
            copies.append(copy)
            arrivals[name, dim, up] = copy

    def receive(name):
        for dim in range(3):
            for up in (1, 0):
                arrivals[name, dim, up].wait_recv()

    def offset(field, z, stride):
        return field * NZ + z * stride

    def packed(current, value, up, field, z, stride):
        at = offset(field, z, stride)
        moved = rolled(value, at + stride if up else at, 1)
        return jnp.where((lane >= at) & (lane < at + stride), moved, current)

    def halo_y(name, up, field, z):
        on = low_on[1] if up else high_on[1]
        return ref[f"recv_{name}_1{up}"][field, z : z + 1, :] * on

    def halo_x(name, up, field, z, stride):
        at = offset(field, z, stride)
        pack = ref[f"recv_{name}_2{up}"][...] * (low_on[2] if up else high_on[2])
        return rolled(pack, NX - at if up else 2 * NX - stride - at, 1)

    def halo_z(name, up, field):
        return ref[f"recv_{name}_0{up}"][field] * (low_on[0] if up else high_on[0])

    def at_low(dim, value, stride):
        return jnp.where((row if dim == 1 else lane) < stride, value, 0.0)

    def at_high(dim, value, stride):
        return jnp.where((row if dim == 1 else lane) >= PLANE[dim - 1] - stride, value, 0.0)

    def from_low(dim, value, stride):
        return jnp.where(
            (row if dim == 1 else lane) < stride, 0.0, rolled(value, stride, dim - 1)
        )

    def from_high(dim, value, stride):
        size = PLANE[dim - 1]
        return jnp.where(
            (row if dim == 1 else lane) >= size - stride, 0.0, rolled(value, -stride, dim - 1)
        )

    trans, blocks, inverses = ref["in_trans"], ref["in_blocks"], ref["in_inverses"]
    iterate, rhs, total = ref["iterate"], ref["rhs"], ref["total"]

    def smoothed(residual, z):
        return [
            inverses[c, z] * residual[0]
            + inverses[3 + c, z] * residual[1]
            + inverses[6 + c, z] * residual[2]
            for c in range(3)
        ]

    def send_iterate(name, channels):
        first = name == "first"
        for c in range(channels):
            ref[f"send_{name}_01"][c] = trans[0, NZ - 1] * iterate[c, NZ - 1]
            ref[f"send_{name}_00"][c] = iterate[c, 0]
        if first:
            ref[f"send_{name}_01"][channels] = trans[0, NZ - 1]
        send(name, 0)
        for z in range(NZ):
            coef = trans[1, z, NY - 1 : NY, :]
            for c in range(channels):
                ref[f"send_{name}_11"][c, z : z + 1, :] = coef * iterate[c, z, NY - 1 : NY, :]
                ref[f"send_{name}_10"][c, z : z + 1, :] = iterate[c, z, 0:1, :]
            if first:
                ref[f"send_{name}_11"][channels, z : z + 1, :] = coef
        send(name, 1)
        high, low = zero, zero
        for z in range(NZ):
            coef = trans[2, z]
            for c in range(channels):
                high = packed(high, coef * iterate[c, z], 1, c, z, 1)
                low = packed(low, iterate[c, z], 0, c, z, 1)
            if first:
                high = packed(high, coef, 1, channels, z, 1)
        ref[f"send_{name}_21"][...] = high
        ref[f"send_{name}_20"][...] = low
        send(name, 2)

    def system_inside(channels):
        for z in range(NZ):
            values = [iterate[c, z] for c in range(3)]
            for c in range(channels):
                value = values[c]
                acc = (
                    blocks[c, z] * values[0]
                    + blocks[3 + c, z] * values[1]
                    + blocks[6 + c, z] * values[2]
                )
                if z > 0:
                    acc = acc - trans[0, z - 1] * iterate[c, z - 1]
                if z < NZ - 1:
                    acc = acc - trans[0, z] * iterate[c, z + 1]
                for dim in (1, 2):
                    coef = trans[dim, z]
                    acc = acc - from_low(dim, coef * value, 1)
                    acc = acc - coef * from_high(dim, value, 1)
                total[c, z] = acc

    def system_row(name, c, z):
        acc = total[c, z] + ref["trans_sum"][z] * iterate[c, z]
        if z == 0:
            acc = acc - halo_z(name, 1, c)
        if z == NZ - 1:
            acc = acc - trans[0, z] * halo_z(name, 0, c)
        acc = acc - at_low(1, halo_y(name, 1, c, z), 1)
        acc = acc - at_high(1, trans[1, z] * halo_y(name, 0, c, z), 1)
        acc = acc - at_low(2, halo_x(name, 1, c, z, 1), 1)
        acc = acc - at_high(2, trans[2, z] * halo_x(name, 0, c, z, 1), 1)
        return acc

    def trans_sum_inside():
        for z in range(NZ):
            acc = trans[0, z] + trans[1, z] + trans[2, z]
            if z > 0:
                acc = acc + trans[0, z - 1]
            for dim in (1, 2):
                acc = acc + from_low(dim, trans[dim, z], 1)
            ref["trans_sum"][z] = acc

    def trans_sum_rims():
        for z in range(NZ):
            acc = ref["trans_sum"][z]
            if z == 0:
                acc = acc + halo_z("first", 1, 3)
            acc = acc + at_low(1, halo_y("first", 1, 3, z), 1)
            acc = acc + at_low(2, halo_x("first", 1, 3, z, 1), 1)
            ref["trans_sum"][z] = acc

    def coef(level, k, z):
        return ref["in_fine"][k, z] if level == 0 else ref[f"coef{level}"][k, z]

    def spread_level(level):
        rows, lanes = NY >> level, NX >> level
        source = ref["in_" + ("one", "two", "three")[level - 1]]
        pick = lax.broadcasted_iota(jnp.int32, (8, NX), 1) // (1 << level)
        for z in range(NZ >> level):
            for k in range(7):
                value = source[k, z]
                value = jnp.concatenate([value] * (1 << level), axis=1)
                if rows < 8:
                    value = jnp.concatenate([value] * (8 // rows), axis=0)
                value = jnp.take_along_axis(value, pick, axis=1, mode="promise_in_bounds")
                wide = jnp.broadcast_to(value[0:1], PLANE)
                for y in range(1, rows):
                    wide = jnp.where(row < y << level, wide, jnp.broadcast_to(value[y : y + 1], PLANE))
                ref[f"coef{level}"][k, z] = wide

    def scales(level):
        for z in range(NZ >> level):
            ref[f"scale{level}"][z] = OMEGA / coef(level, 0, z)

    def send_level(name, level):
        planes, stride = NZ >> level, 1 << level
        x = ref[f"x{level}"]
        ref[f"send_{name}_01"][0] = coef(level, 2, planes - 1) * x[planes - 1]
        ref[f"send_{name}_00"][0] = coef(level, 1, 0) * x[0]
        send(name, 0)
        for z in range(planes):
            ref[f"send_{name}_11"][0, z : z + 1, :] = (coef(level, 4, z) * x[z])[NY - 1 : NY]
            ref[f"send_{name}_10"][0, z : z + 1, :] = (coef(level, 3, z) * x[z])[0:1]
        send(name, 1)
        high, low = zero, zero
        for z in range(planes):
            high = packed(high, coef(level, 6, z) * x[z], 1, 0, z, stride)
            low = packed(low, coef(level, 5, z) * x[z], 0, 0, z, stride)
        ref[f"send_{name}_21"][...] = high
        ref[f"send_{name}_20"][...] = low
        send(name, 2)

    def residual_inside(level):
        planes, stride = NZ >> level, 1 << level
        x, b, r = ref[f"x{level}"], ref[f"b{level}"], ref[f"r{level}"]
        for z in range(planes):
            acc = b[z] - coef(level, 0, z) * x[z]
            if z > 0:
                acc = acc - coef(level, 2, z - 1) * x[z - 1]
            if z < planes - 1:
                acc = acc - coef(level, 1, z + 1) * x[z + 1]
            for dim in (1, 2):
                acc = acc - from_low(dim, coef(level, 2 * dim + 2, z) * x[z], stride)
                acc = acc - from_high(dim, coef(level, 2 * dim + 1, z) * x[z], stride)
            r[z] = acc

    def residual(name, level, z):
        planes, stride = NZ >> level, 1 << level
        acc = ref[f"r{level}"][z]
        if z == 0:
            acc = acc - halo_z(name, 1, 0)
        if z == planes - 1:
            acc = acc - halo_z(name, 0, 0)
        acc = acc - at_low(1, halo_y(name, 1, 0, z), stride)
        acc = acc - at_high(1, halo_y(name, 0, 0, z), stride)
        acc = acc - at_low(2, halo_x(name, 1, 0, z, stride), stride)
        acc = acc - at_high(2, halo_x(name, 0, 0, z, stride), stride)
        return acc

    def paired(value, stride):
        for dim, place in ((0, row), (1, lane)):
            upper = (place & stride) != 0
            value = value + jnp.where(
                upper, rolled(value, stride, dim), rolled(value, -stride, dim)
            )
        return value

    def relax(name, level):
        send_level(name, level)
        residual_inside(level)
        receive(name)
        for z in range(NZ >> level):
            ref[f"x{level}"][z] = ref[f"x{level}"][z] + ref[f"scale{level}"][z] * residual(
                name, level, z
            )

    def start_level(level):
        for z in range(NZ >> level):
            ref[f"x{level}"][z] = ref[f"scale{level}"][z] * ref[f"b{level}"][z]

    saved, pressure = ref["in_mobilities"], ref["in_pressure"]

    def send_saved():
        name = "saved"
        fields = [lambda z, c=c: saved[c, z] for c in range(3)] + [lambda z: pressure[z]]
        for f, field in enumerate(fields):
            ref[f"send_{name}_01"][f] = field(NZ - 1)
            ref[f"send_{name}_00"][f] = field(0)
        send(name, 0)
        for f, field in enumerate(fields):
            for z in range(NZ):
                ref[f"send_{name}_11"][f, z : z + 1, :] = field(z)[NY - 1 : NY]
                ref[f"send_{name}_10"][f, z : z + 1, :] = field(z)[0:1]
        send(name, 1)
        high, low = zero, zero
        for f, field in enumerate(fields):
            for z in range(NZ):
                high = packed(high, field(z), 1, f, z, 1)
                low = packed(low, field(z), 0, f, z, 1)
        ref[f"send_{name}_21"][...] = high
        ref[f"send_{name}_20"][...] = low
        send(name, 2)

    def face_weights():
        name = "saved"
        receive(name)
        for z in range(NZ):
            p = pressure[z]
            for dim in range(3):
                if dim == 0:
                    high = pressure[z + 1] if z < NZ - 1 else halo_z(name, 0, 3)
                elif dim == 1:
                    high = from_high(1, p, 1) + at_high(1, halo_y(name, 0, 3, z), 1)
                else:
                    high = from_high(2, p, 1) + at_high(2, halo_x(name, 0, 3, z, 1), 1)
                step = 0.25 * trans[dim, z] * (p - high)
                for c in range(3):
                    m = saved[c, z]
                    if dim == 0:
                        high = saved[c, z + 1] if z < NZ - 1 else halo_z(name, 0, c)
                    elif dim == 1:
                        high = from_high(1, m, 1) + at_high(1, halo_y(name, 0, c, z), 1)
                    else:
                        high = from_high(2, m, 1) + at_high(2, halo_x(name, 0, c, z, 1), 1)
                    ref["face"][dim, c, z] = step * (m + high)
            step = 0.25 * halo_y("first", 1, 3, z) * (halo_y(name, 1, 3, z) - p[0:1])
            for c in range(3):
                ref["face_low_y"][c, z : z + 1, :] = step * (
                    halo_y(name, 1, c, z) + saved[c, z, 0:1, :]
                )
            step = 0.25 * halo_x("first", 1, 3, z, 1) * (halo_x(name, 1, 3, z, 1) - p)
            for c in range(3):
                ref["face_low_x"][c, z] = step * (halo_x(name, 1, c, z, 1) + saved[c, z])
        step = 0.25 * halo_z("first", 1, 3) * (halo_z(name, 1, 3) - pressure[0])
        for c in range(3):
            ref["face_low_z"][c] = step * (halo_z(name, 1, c) + saved[c, 0])

    loads["source"].wait()
    loads["active"].wait()
    loads["inverses"].wait()
    for z in range(NZ):
        mask = ref["in_active"][z].astype(jnp.float32)
        values = [ref["in_source"][c, z] * mask for c in range(3)]
        for c in range(3):
            rhs[c, z] = values[c]
        for c, value in enumerate(smoothed(values, z)):
            iterate[c, z] = value
    loads["trans"].wait()
    pl.semaphore_wait(barrier, 6)

    for name, channels in (("first", 3), ("second", 3), ("third", 1)):
        send_iterate(name, channels)
        if name == "first":
            loads["blocks"].wait()
        system_inside(channels)
        if name == "first":
            trans_sum_inside()
            loads["mobilities"].wait()
            loads["pressure"].wait()
            send_saved()
        elif name == "second":
            for load in ("fine", "one", "two", "three"):
                loads[load].wait()
            scales(0)
            spread_level(1)
            scales(1)
        else:
            for level in (2, 3):
                spread_level(level)
                scales(level)
        receive(name)
        if name == "first":
            trans_sum_rims()
        for z in range(NZ):
            if name == "third":
                value = rhs[0, z] - system_row(name, 0, z)
                ref["b0"][z] = value
                ref["x0"][z] = ref["scale0"][z] * value
            else:
                left = [rhs[c, z] - system_row(name, c, z) for c in range(3)]
                for c, value in enumerate(smoothed(left, z)):
                    iterate[c, z] = iterate[c, z] + value

    for level in range(LEVELS):
        name = f"down{level}"
        send_level(name, level)
        residual_inside(level)
        if level == 1:
            face_weights()
        receive(name)
        for z in range(NZ >> (level + 1)):
            pair = residual(name, level, 2 * z) + residual(name, level, 2 * z + 1)
            value = paired(pair, 1 << level)
            ref[f"b{level + 1}"][z] = value
            ref[f"x{level + 1}"][z] = ref[f"scale{level + 1}"][z] * value
    for sweep in range(COARSE_SWEEPS - 1):
        relax(f"base{sweep}", LEVELS)
    for level in reversed(range(LEVELS)):
        for z in range(NZ >> level):
            ref[f"x{level}"][z] = ref[f"x{level}"][z] + ref[f"x{level + 1}"][z // 2]
        relax(f"up{level}", level)

    loads["weights"].wait()
    name = "last"
    for z in range(NZ):
        mask = ref["in_active"][z].astype(jnp.float32)
        for c in range(3):
            adjoint_ref[c, z] = mask * (iterate[c, z] + ref["in_weights"][c, z] * ref["x0"][z])
    for c in range(3):
        ref[f"send_{name}_01"][c] = adjoint_ref[c, NZ - 1]
        ref[f"send_{name}_00"][c] = adjoint_ref[c, 0]
    send(name, 0)
    for z in range(NZ):
        for c in range(3):
            ref[f"send_{name}_11"][c, z : z + 1, :] = adjoint_ref[c, z, NY - 1 : NY, :]
            ref[f"send_{name}_10"][c, z : z + 1, :] = adjoint_ref[c, z, 0:1, :]
    send(name, 1)
    high, low = zero, zero
    for z in range(NZ):
        for c in range(3):
            high = packed(high, adjoint_ref[c, z], 1, c, z, 1)
            low = packed(low, adjoint_ref[c, z], 0, c, z, 1)
    ref[f"send_{name}_21"][...] = high
    ref[f"send_{name}_20"][...] = low
    send(name, 2)

    face = ref["face"]
    for dim in range(3):
        previous = None
        for z in range(NZ):
            flux = None
            for c in range(3):
                value = adjoint_ref[c, z]
                if dim == 0:
                    drop = value - adjoint_ref[c, z + 1] if z < NZ - 1 else value
                else:
                    drop = value - from_high(dim, value, 1)
                term = face[dim, c, z] * drop
                flux = term if flux is None else flux + term
            if dim == 0:
                gradient_ref[dim, z] = flux if previous is None else flux + previous
                previous = flux
            else:
                gradient_ref[dim, z] = flux + from_low(dim, flux, 1)
    receive(name)
    low_z, high_z = zero, zero
    for c in range(3):
        low_z = low_z + ref["face_low_z"][c] * (halo_z(name, 1, c) - adjoint_ref[c, 0])
        high_z = high_z + face[0, c, NZ - 1] * halo_z(name, 0, c)
    gradient_ref[0, 0] = gradient_ref[0, 0] + low_z
    gradient_ref[0, NZ - 1] = gradient_ref[0, NZ - 1] - high_z
    for z in range(NZ):
        low_y, high_y, low_x, high_x = zero, zero, zero, zero
        for c in range(3):
            value = adjoint_ref[c, z]
            low_y = low_y + ref["face_low_y"][c, z : z + 1, :] * (halo_y(name, 1, c, z) - value)
            high_y = high_y + face[1, c, z] * halo_y(name, 0, c, z)
            low_x = low_x + ref["face_low_x"][c, z] * (halo_x(name, 1, c, z, 1) - value)
            high_x = high_x + face[2, c, z] * halo_x(name, 0, c, z, 1)
        gradient_ref[1, z] = gradient_ref[1, z] + at_low(1, low_y, 1) - at_high(1, high_y, 1)
        gradient_ref[2, z] = gradient_ref[2, z] + at_low(2, low_x, 1) - at_high(2, high_x, 1)

    for copy in copies:
        copy.wait_send()


def solution(mesh):
    sizes = [mesh.shape[axis] for axis in AXES]

    def local(*args):
        shapes = {name: (arg.shape, arg.dtype) for name, arg in zip(INPUTS, args)}
        table = scratch_table(shapes)
        out = jax.ShapeDtypeStruct((3, NZ) + PLANE, jnp.float32)
        return pl.pallas_call(
            functools.partial(kernel, sizes, tuple(table)),
            out_shape=(out, out),
            in_specs=[pl.BlockSpec(memory_space=pl.ANY)] * len(INPUTS),
            out_specs=(pl.BlockSpec(memory_space=pltpu.VMEM),) * 2,
            scratch_shapes=list(table.values()),
            compiler_params=pltpu.CompilerParams(collective_id=0, has_side_effects=True),
        )(*args)

    field = P("layer", "gy", "gx")
    stacked = P(None, "layer", "gy", "gx")
    return jax.shard_map(
        local,
        mesh=mesh,
        in_specs=(stacked, field) + (stacked,) * 8 + (field, stacked),
        out_specs=(stacked, stacked),
        check_vma=False,
    )
```

```python
import functools

import jax
import jax.numpy as jnp
from jax import lax
from jax.experimental import pallas as pl
from jax.experimental.pallas import tpu as pltpu
from jax.sharding import PartitionSpec as P

MESH = pl.DeviceIdType.MESH
OMEGA = 0.8
COARSE_SWEEPS = 4
AXES = ("layer", "gy", "gx")
NZ, NY, NX = 8, 16, 128
PLANE = (NY, NX)

FIRST, SECOND, THIRD, SAVED, RIMS, DOWN0, DOWN1, UP0, LAST = range(9)
ROUNDS = (
    (4, 3, 8),
    (3, 3, 8),
    (1, 1, 8),
    (4, 4, 8),
    (1, 1, 4),
    (1, 1, 8),
    (1, 1, 4),
    (1, 1, 8),
    (3, 3, 8),
)

(SOURCE, ACTIVE, BLOCKS, INVERSES, TRANS, WEIGHTS, FINE, ONE, TWO, THREE, PRESSURE, MOBILITIES) = range(12)
LOAD_ORDER = (SOURCE, ACTIVE, INVERSES, TRANS, BLOCKS, TWO, THREE, ONE, FINE, MOBILITIES, PRESSURE, WEIGHTS)

(
    LOADED,
    SEND,
    RECV,
    RHS,
    ITERATE,
    TOTAL,
    TRANS_SUM,
    COEF,
    SCALE,
    B,
    X,
    R,
    FACE,
    FACE_LOW,
    OWN_COEF,
    ALL_COEF,
    OWN_B,
    ALL_B,
    WIDE_COEF,
    WIDE_SCALE,
    WIDE_B,
    WIDE_X,
    WIDE_R,
    LOAD_SEM,
    SEND_SEM,
    RECV_SEM,
    COEF_SEM,
    B_SEM,
) = range(28)

WIDE = (32, 128)
REACH_Y = 3
PEERS = tuple(
    (a, b, c)
    for b in range(-REACH_Y, REACH_Y + 1)
    for a in (-1, 0, 1)
    for c in range(4)
    if (a, b, c) != (0, 0, 0)
    and (abs(b) < 3 or (a == 0 and c == 0))
    and (abs(b) < 2 or a == 0 or c != 2)
)


def message_shape(name, dim, up):
    fields_up, fields_down, planes = ROUNDS[name]
    fields = fields_up if up else fields_down
    if dim == 0:
        return (fields, NY, NX)
    if dim == 1:
        return (fields, planes, NX)
    return PLANE


def scratch_table(shapes):
    def vmem(*shape):
        return pltpu.VMEM(shape, jnp.float32)

    table = {}
    for name, (shape, dtype) in enumerate(shapes):
        table[LOADED, name] = pltpu.VMEM(shape, dtype)
    for name in (RHS, ITERATE, TOTAL):
        table[name] = vmem(3, NZ, *PLANE)
    table[TRANS_SUM] = vmem(NZ, *PLANE)
    for level in (0, 1):
        planes = NZ >> level
        if level:
            table[COEF, level] = vmem(7, planes, *PLANE)
        for name in (SCALE, B, X, R):
            table[name, level] = vmem(planes, *PLANE)
    table[FACE] = vmem(3, 3, NZ, *PLANE)
    table[FACE_LOW, 0] = vmem(3, *PLANE)
    table[FACE_LOW, 1] = vmem(3, NZ, NX)
    table[FACE_LOW, 2] = vmem(3, NZ, *PLANE)
    table[OWN_COEF] = vmem(16, NX)
    table[ALL_COEF] = vmem(3, 4, 2 * REACH_Y + 1, 16, NX)
    table[OWN_B] = vmem(2, NX)
    table[ALL_B] = vmem(3, 4, 2 * REACH_Y + 1, 2, NX)
    for level in (2, 3):
        planes = 16 >> (level - 1)
        table[WIDE_COEF, level] = vmem(7, planes, *WIDE)
        for name in (WIDE_SCALE, WIDE_B, WIDE_R):
            table[name, level] = vmem(planes, *WIDE)
        table[WIDE_X, level] = vmem(planes + 2, *WIDE)
    for name in range(len(ROUNDS)):
        for dim in range(3):
            for up in (0, 1):
                table[SEND, name, dim, up] = vmem(*message_shape(name, dim, up))
                table[RECV, name, dim, up] = vmem(*message_shape(name, dim, up))
    table[LOAD_SEM] = pltpu.SemaphoreType.DMA((len(shapes),))
    for name, count in ((SEND_SEM, 6 * len(ROUNDS)), (RECV_SEM, 6 * len(ROUNDS))):
        table[name] = pltpu.SemaphoreType.DMA((count,))
    for name in (COEF_SEM, B_SEM):
        table[name] = pltpu.SemaphoreType.DMA((2, len(PEERS)))
    return table


def rolled(value, amount, axis):
    amount = amount % value.shape[axis]
    return pltpu.roll(value, amount, axis) if amount else value


def kernel(sizes, scratch_names, *refs):
    hbm = refs[:12]
    adjoint_ref, gradient_ref = refs[12:14]
    ref = dict(zip(scratch_names, refs[14:]))

    me = [lax.axis_index(axis) for axis in AXES]
    above = [lax.rem(me[d] + 1, sizes[d]) for d in range(3)]
    below = [lax.rem(me[d] + sizes[d] - 1, sizes[d]) for d in range(3)]

    loads = {}
    for name in LOAD_ORDER:
        loads[name] = pltpu.make_async_copy(
            hbm[name], ref[LOADED, name], ref[LOAD_SEM].at[name]
        )
        loads[name].start()

    for dx in range(3):
        for layer in range(4):
            for dy in range(2 * REACH_Y + 1):
                ref[ALL_COEF][dx, layer, dy] = jnp.zeros((16, NX), jnp.float32)
                ref[ALL_B][dx, layer, dy] = jnp.zeros((2, NX), jnp.float32)

    def peer_of(offset):
        a, b, c = offset
        return (
            lax.rem(me[2] + (a + sizes[2]), sizes[2]),
            lax.rem(me[1] + (b + sizes[1]), sizes[1]),
            lax.rem(me[0] + c, sizes[0]),
        )

    barrier = pltpu.get_barrier_semaphore()
    for offset in PEERS:
        pl.semaphore_signal(barrier, inc=1, device_id=peer_of(offset), device_id_type=MESH)

    low_on = [jnp.where(me[d] > 0, 1.0, 0.0).astype(jnp.float32) for d in range(3)]
    high_on = [jnp.where(me[d] < sizes[d] - 1, 1.0, 0.0).astype(jnp.float32) for d in range(3)]

    row = lax.broadcasted_iota(jnp.int32, PLANE, 0)
    lane = lax.broadcasted_iota(jnp.int32, PLANE, 1)
    zero = jnp.zeros(PLANE, jnp.float32)
    copies = []
    arrivals = {}

    def send(name, dim):
        for up in (1, 0):
            k = name * 6 + dim * 2 + up
            copy = pltpu.make_async_remote_copy(
                src_ref=ref[SEND, name, dim, up],
                dst_ref=ref[RECV, name, dim, up],
                send_sem=ref[SEND_SEM].at[k],
                recv_sem=ref[RECV_SEM].at[k],
                device_id={AXES[dim]: above[dim] if up else below[dim]},
                device_id_type=MESH,
            )
            copy.start()
            copies.append(copy)
            arrivals[name, dim, up] = copy

    def receive(name):
        for dim in range(3):
            for up in (1, 0):
                arrivals[name, dim, up].wait_recv()

    def offset(field, z, stride):
        return field * NZ + z * stride

    def packed(current, value, up, field, z, stride):
        at = offset(field, z, stride)
        moved = rolled(value, at + stride if up else at, 1)
        return jnp.where((lane >= at) & (lane < at + stride), moved, current)

    def halo_y(name, up, field, z):
        on = low_on[1] if up else high_on[1]
        return ref[RECV, name, 1, up][field, z : z + 1, :] * on

    def halo_x(name, up, field, z, stride):
        at = offset(field, z, stride)
        pack = ref[RECV, name, 2, up][...] * (low_on[2] if up else high_on[2])
        return rolled(pack, NX - at if up else 2 * NX - stride - at, 1)

    def halo_z(name, up, field):
        return ref[RECV, name, 0, up][field] * (low_on[0] if up else high_on[0])

    def at_low(dim, value, stride):
        return jnp.where((row if dim == 1 else lane) < stride, value, 0.0)

    def at_high(dim, value, stride):
        return jnp.where((row if dim == 1 else lane) >= PLANE[dim - 1] - stride, value, 0.0)

    def from_low(dim, value, stride):
        return jnp.where(
            (row if dim == 1 else lane) < stride, 0.0, rolled(value, stride, dim - 1)
        )

    def from_high(dim, value, stride):
        size = PLANE[dim - 1]
        return jnp.where(
            (row if dim == 1 else lane) >= size - stride, 0.0, rolled(value, -stride, dim - 1)
        )

    trans, blocks, inverses = ref[LOADED, TRANS], ref[LOADED, BLOCKS], ref[LOADED, INVERSES]
    iterate, rhs, total = ref[ITERATE], ref[RHS], ref[TOTAL]

    def smoothed(residual, z):
        return [
            inverses[c, z] * residual[0]
            + inverses[3 + c, z] * residual[1]
            + inverses[6 + c, z] * residual[2]
            for c in range(3)
        ]

    def send_iterate(name, channels):
        first = name == FIRST
        for c in range(channels):
            ref[SEND, name, 0, 1][c] = trans[0, NZ - 1] * iterate[c, NZ - 1]
            ref[SEND, name, 0, 0][c] = iterate[c, 0]
        if first:
            ref[SEND, name, 0, 1][channels] = trans[0, NZ - 1]
        send(name, 0)
        for z in range(NZ):
            coef = trans[1, z, NY - 1 : NY, :]
            for c in range(channels):
                ref[SEND, name, 1, 1][c, z : z + 1, :] = coef * iterate[c, z, NY - 1 : NY, :]
                ref[SEND, name, 1, 0][c, z : z + 1, :] = iterate[c, z, 0:1, :]
            if first:
                ref[SEND, name, 1, 1][channels, z : z + 1, :] = coef
        send(name, 1)
        high, low = zero, zero
        for z in range(NZ):
            coef = trans[2, z]
            for c in range(channels):
                high = packed(high, coef * iterate[c, z], 1, c, z, 1)
                low = packed(low, iterate[c, z], 0, c, z, 1)
            if first:
                high = packed(high, coef, 1, channels, z, 1)
        ref[SEND, name, 2, 1][...] = high
        ref[SEND, name, 2, 0][...] = low
        send(name, 2)

    def system_inside(channels):
        for z in range(NZ):
            values = [iterate[c, z] for c in range(3)]
            for c in range(channels):
                value = values[c]
                acc = (
                    blocks[c, z] * values[0]
                    + blocks[3 + c, z] * values[1]
                    + blocks[6 + c, z] * values[2]
                )
                if z > 0:
                    acc = acc - trans[0, z - 1] * iterate[c, z - 1]
                if z < NZ - 1:
                    acc = acc - trans[0, z] * iterate[c, z + 1]
                for dim in (1, 2):
                    coef = trans[dim, z]
                    acc = acc - from_low(dim, coef * value, 1)
                    acc = acc - coef * from_high(dim, value, 1)
                total[c, z] = acc

    def system_row(name, c, z):
        acc = total[c, z] + ref[TRANS_SUM][z] * iterate[c, z]
        if z == 0:
            acc = acc - halo_z(name, 1, c)
        if z == NZ - 1:
            acc = acc - trans[0, z] * halo_z(name, 0, c)
        acc = acc - at_low(1, halo_y(name, 1, c, z), 1)
        acc = acc - at_high(1, trans[1, z] * halo_y(name, 0, c, z), 1)
        acc = acc - at_low(2, halo_x(name, 1, c, z, 1), 1)
        acc = acc - at_high(2, trans[2, z] * halo_x(name, 0, c, z, 1), 1)
        return acc

    def trans_sum_inside():
        for z in range(NZ):
            acc = trans[0, z] + trans[1, z] + trans[2, z]
            if z > 0:
                acc = acc + trans[0, z - 1]
            for dim in (1, 2):
                acc = acc + from_low(dim, trans[dim, z], 1)
            ref[TRANS_SUM][z] = acc

    def trans_sum_rims():
        for z in range(NZ):
            acc = ref[TRANS_SUM][z]
            if z == 0:
                acc = acc + halo_z(FIRST, 1, 3)
            acc = acc + at_low(1, halo_y(FIRST, 1, 3, z), 1)
            acc = acc + at_low(2, halo_x(FIRST, 1, 3, z, 1), 1)
            ref[TRANS_SUM][z] = acc

    def coef(level, k, z):
        return ref[LOADED, FINE][k, z] if level == 0 else ref[COEF, level][k, z]

    def spread_level(level):
        rows, lanes = NY >> level, NX >> level
        source = ref[LOADED, ONE]
        pick = lax.broadcasted_iota(jnp.int32, (8, NX), 1) // (1 << level)
        for z in range(NZ >> level):
            for k in range(7):
                value = source[k, z]
                value = jnp.concatenate([value] * (1 << level), axis=1)
                if rows < 8:
                    value = jnp.concatenate([value] * (8 // rows), axis=0)
                value = jnp.take_along_axis(value, pick, axis=1, mode="promise_in_bounds")
                wide = jnp.broadcast_to(value[0:1], PLANE)
                for y in range(1, rows):
                    wide = jnp.where(row < y << level, wide, jnp.broadcast_to(value[y : y + 1], PLANE))
                ref[COEF, level][k, z] = wide

    def scales(level):
        for z in range(NZ >> level):
            ref[SCALE, level][z] = OMEGA / coef(level, 0, z)

    def send_level(name, level):
        planes, stride = NZ >> level, 1 << level
        x = [1.0] * planes if name == RIMS else ref[X, level]
        ref[SEND, name, 0, 1][0] = coef(level, 2, planes - 1) * x[planes - 1]
        ref[SEND, name, 0, 0][0] = coef(level, 1, 0) * x[0]
        send(name, 0)
        for z in range(planes):
            ref[SEND, name, 1, 1][0, z : z + 1, :] = (coef(level, 4, z) * x[z])[NY - 1 : NY]
            ref[SEND, name, 1, 0][0, z : z + 1, :] = (coef(level, 3, z) * x[z])[0:1]
        send(name, 1)
        high, low = zero, zero
        for z in range(planes):
            high = packed(high, coef(level, 6, z) * x[z], 1, 0, z, stride)
            low = packed(low, coef(level, 5, z) * x[z], 0, 0, z, stride)
        ref[SEND, name, 2, 1][...] = high
        ref[SEND, name, 2, 0][...] = low
        send(name, 2)

    def residual_inside(level):
        planes, stride = NZ >> level, 1 << level
        x, b, r = ref[X, level], ref[B, level], ref[R, level]
        for z in range(planes):
            acc = b[z] - coef(level, 0, z) * x[z]
            if z > 0:
                acc = acc - coef(level, 2, z - 1) * x[z - 1]
            if z < planes - 1:
                acc = acc - coef(level, 1, z + 1) * x[z + 1]
            for dim in (1, 2):
                acc = acc - from_low(dim, coef(level, 2 * dim + 2, z) * x[z], stride)
                acc = acc - from_high(dim, coef(level, 2 * dim + 1, z) * x[z], stride)
            r[z] = acc

    def residual(name, level, z):
        planes, stride = NZ >> level, 1 << level
        acc = ref[R, level][z]
        if z == 0:
            acc = acc - halo_z(name, 1, 0)
        if z == planes - 1:
            acc = acc - halo_z(name, 0, 0)
        acc = acc - at_low(1, halo_y(name, 1, 0, z), stride)
        acc = acc - at_high(1, halo_y(name, 0, 0, z), stride)
        acc = acc - at_low(2, halo_x(name, 1, 0, z, stride), stride)
        acc = acc - at_high(2, halo_x(name, 0, 0, z, stride), stride)
        return acc

    def paired(value, stride):
        for dim, place in ((0, row), (1, lane)):
            upper = (place & stride) != 0
            value = value + jnp.where(
                upper, rolled(value, stride, dim), rolled(value, -stride, dim)
            )
        return value

    row8 = lax.broadcasted_iota(jnp.int32, (8, NX), 0)
    lane8 = lax.broadcasted_iota(jnp.int32, (8, NX), 1)
    lane1 = lax.broadcasted_iota(jnp.int32, (1, NX), 1)
    windows = 2 * REACH_Y + 1

    def along_lanes(value, index):
        return jnp.take_along_axis(value, index, axis=1, mode="promise_in_bounds")

    def pack_own_coef():
        for k in range(7):
            place = lax.broadcasted_iota(jnp.int32, (4, NX), 0)
            lanes = lax.broadcasted_iota(jnp.int32, (4, NX), 1)
            for z in range(2):
                value = jnp.concatenate([ref[LOADED, TWO][k, z]] * 4, axis=1)
                value = jnp.where(lanes // 32 == place, value, 0.0)
                at = 2 * k + z
                ref[OWN_COEF][at : at + 1, :] = jnp.sum(value, axis=0, keepdims=True)
        place = lax.broadcasted_iota(jnp.int32, (2, NX), 0)
        lanes = lax.broadcasted_iota(jnp.int32, (2, NX), 1)
        for half in range(2):
            packed_row = jnp.zeros((1, NX), jnp.float32)
            for k in range(4 * half, min(7, 4 * half + 4)):
                value = jnp.concatenate([ref[LOADED, THREE][k, 0]] * 8, axis=1)
                value = jnp.where((lanes % 32) // 16 == place, value, 0.0)
                value = jnp.sum(value, axis=0, keepdims=True)
                packed_row = jnp.where(lane1 // 32 == k % 4, value, packed_row)
            ref[OWN_COEF][14 + half : 15 + half, :] = packed_row
        ref[ALL_COEF][1, me[0], REACH_Y] = ref[OWN_COEF][...]

    def pack_own_b(planes):
        for z, plane in enumerate(planes):
            total_row = jnp.zeros((8, NX), jnp.float32)
            for half in range(2):
                value = along_lanes(plane[8 * half : 8 * half + 8], 4 * (lane8 % 32))
                keep = (row8 % 4 == 0) & (row8 // 4 + 2 * half == lane8 // 32)
                total_row = total_row + jnp.where(keep, value, 0.0)
            ref[OWN_B][z : z + 1, :] = jnp.sum(total_row, axis=0, keepdims=True)
        ref[ALL_B][1, me[0], REACH_Y] = ref[OWN_B][...]

    def spread_to_peers(own, everyone, sems, chosen):
        for i in chosen:
            a, b, c = PEERS[i]
            copy = pltpu.make_async_remote_copy(
                src_ref=ref[own],
                dst_ref=ref[everyone].at[1 - a, me[0], REACH_Y - b],
                send_sem=ref[sems].at[0, i],
                recv_sem=ref[sems].at[1, i],
                device_id=peer_of(PEERS[i]),
                device_id_type=MESH,
            )
            copy.start()
            copies.append(copy)
            arrivals[sems, i] = copy

    def receive_from_peers(sems):
        for i in range(len(PEERS)):
            arrivals[sems, i].wait_recv()

    def inside(value, size):
        return jnp.where((value >= 0) & (value < size), 1.0, 0.0).astype(jnp.float32)

    in_y = [inside(me[1] + (dy - REACH_Y), sizes[1]) for dy in range(windows)]
    in_x = [inside(me[2] + (dx - 1), sizes[2]) for dx in range(3)]

    def unpacked(everyone, layer, at, level, base, masked):
        width, rows = (32, row8 % 4) if level == 2 else (16, row8 % 4 // 2)
        step = 2 if level == 2 else 4
        start = base + rows * width
        middle = start + (lane8 - 32) // step
        sides = start + jnp.where(lane8 < 32, width // 2 + lane8 // step, (lane8 - 96) // step)
        tiles = []
        for t in range(4):
            halves = []
            for dy in (2 * t, 2 * t + 1):
                if dy >= windows:
                    blank = jnp.zeros((1, NX), jnp.float32)
                    halves.append((blank, blank))
                    continue
                left, own, right = [
                    ref[everyone][dx, layer, dy, at : at + 1, :] for dx in range(3)
                ]
                if masked:
                    left, own, right = (
                        left * (in_x[0] * in_y[dy]),
                        own * in_y[dy],
                        right * (in_x[2] * in_y[dy]),
                    )
                halves.append((own, jnp.where(lane1 % width < width // 2, right, left)))
            own, both = [
                jnp.where(
                    row8 < 4,
                    jnp.broadcast_to(halves[0][i], (8, NX)),
                    jnp.broadcast_to(halves[1][i], (8, NX)),
                )
                for i in range(2)
            ]
            tiles.append(
                jnp.where(
                    (lane8 >= 32) & (lane8 < 96),
                    along_lanes(own, jnp.clip(middle, 0, NX - 1)),
                    along_lanes(both, sides),
                )
            )
        return tiles

    def wide_coefs(level):
        for layer in range(4):
            for k in range(7):
                for zz in range(2 if level == 2 else 1):
                    at, base = (2 * k + zz, 0) if level == 2 else (14 + k // 4, k % 4 * 32)
                    plane = 2 * layer + zz if level == 2 else layer
                    for t, tile in enumerate(unpacked(ALL_COEF, layer, at, level, base, True)):
                        ref[WIDE_COEF, level][k, plane, 8 * t : 8 * t + 8, :] = tile
                        if k == 0:
                            live = tile > 0.0
                            ref[WIDE_SCALE, level][plane, 8 * t : 8 * t + 8, :] = jnp.where(
                                live, OMEGA / jnp.where(live, tile, 1.0), 0.0
                            )

    def wide_residual(level, z):
        planes = 16 >> (level - 1)
        rows, lanes = (1, 2) if level == 2 else (2, 4)
        a, x = ref[WIDE_COEF, level], ref[WIDE_X, level]
        acc = ref[WIDE_B, level][z] - a[0, z] * x[z + 1]
        if z > 0:
            acc = acc - a[2, z - 1] * x[z]
        if z < planes - 1:
            acc = acc - a[1, z + 1] * x[z + 2]
        for dim, stride in ((0, rows), (1, lanes)):
            acc = acc - rolled(a[2 * dim + 4, z] * x[z + 1], stride, dim)
            acc = acc - rolled(a[2 * dim + 3, z] * x[z + 1], -stride, dim)
        return acc

    def wide_relax(level):
        planes = 16 >> (level - 1)
        for z in range(planes):
            ref[WIDE_R, level][z] = wide_residual(level, z)
        x = ref[WIDE_X, level]
        for z in range(planes):
            x[z + 1] = x[z + 1] + ref[WIDE_SCALE, level][z] * ref[WIDE_R, level][z]

    def wide_start(level, z, value):
        ref[WIDE_B, level][z] = value
        ref[WIDE_X, level][z + 1] = ref[WIDE_SCALE, level][z] * value

    def wide_solve():
        wide_row = lax.broadcasted_iota(jnp.int32, WIDE, 0)
        wide_lane = lax.broadcasted_iota(jnp.int32, WIDE, 1)
        for layer in range(4):
            for zz in range(2):
                tiles = unpacked(ALL_B, layer, zz, 2, 0, False)
                wide_start(2, 2 * layer + zz, jnp.concatenate(tiles, axis=0))
        for z in range(4):
            pair = wide_residual(2, 2 * z) + wide_residual(2, 2 * z + 1)
            for dim, place, stride in ((0, wide_row, 1), (1, wide_lane, 2)):
                upper = (place & stride) != 0
                pair = pair + jnp.where(
                    upper, rolled(pair, stride, dim), rolled(pair, -stride, dim)
                )
            wide_start(3, z, pair)
        for sweep in range(COARSE_SWEEPS - 1):
            wide_relax(3)
        for z in range(8):
            ref[WIDE_X, 2][z + 1] = ref[WIDE_X, 2][z + 1] + ref[WIDE_X, 3][z // 2 + 1]
        wide_relax(2)

    def onto_fine(wide_plane):
        x = ref[WIDE_X, 2]
        tile = x[wide_plane, 8:16, :]
        after = x[wide_plane, 16:24, :]
        here = 32 + lane8 // 4 * 2

        def rows_of(value):
            wide = jnp.broadcast_to(value[4:5], PLANE)
            for y in range(1, 4):
                wide = jnp.where(row < 4 * y, wide, jnp.broadcast_to(value[4 + y : 5 + y], PLANE))
            return wide

        own = along_lanes(tile, here)
        return (
            rows_of(own),
            own[3:4],
            along_lanes(after, here)[0:1],
            rows_of(along_lanes(tile, 31 + 0 * lane8)),
            rows_of(along_lanes(tile, 96 + 0 * lane8)),
        )

    saved, pressure = ref[LOADED, MOBILITIES], ref[LOADED, PRESSURE]

    def send_saved():
        name = SAVED
        fields = [lambda z, c=c: saved[c, z] for c in range(3)] + [lambda z: pressure[z]]
        for f, field in enumerate(fields):
            ref[SEND, name, 0, 1][f] = field(NZ - 1)
            ref[SEND, name, 0, 0][f] = field(0)
        send(name, 0)
        for f, field in enumerate(fields):
            for z in range(NZ):
                ref[SEND, name, 1, 1][f, z : z + 1, :] = field(z)[NY - 1 : NY]
                ref[SEND, name, 1, 0][f, z : z + 1, :] = field(z)[0:1]
        send(name, 1)
        high, low = zero, zero
        for f, field in enumerate(fields):
            for z in range(NZ):
                high = packed(high, field(z), 1, f, z, 1)
                low = packed(low, field(z), 0, f, z, 1)
        ref[SEND, name, 2, 1][...] = high
        ref[SEND, name, 2, 0][...] = low
        send(name, 2)

    def face_weights():
        name = SAVED
        receive(name)
        for z in range(NZ):
            p = pressure[z]
            for dim in range(3):
                if dim == 0:
                    high = pressure[z + 1] if z < NZ - 1 else halo_z(name, 0, 3)
                elif dim == 1:
                    high = from_high(1, p, 1) + at_high(1, halo_y(name, 0, 3, z), 1)
                else:
                    high = from_high(2, p, 1) + at_high(2, halo_x(name, 0, 3, z, 1), 1)
                step = 0.25 * trans[dim, z] * (p - high)
                for c in range(3):
                    m = saved[c, z]
                    if dim == 0:
                        high = saved[c, z + 1] if z < NZ - 1 else halo_z(name, 0, c)
                    elif dim == 1:
                        high = from_high(1, m, 1) + at_high(1, halo_y(name, 0, c, z), 1)
                    else:
                        high = from_high(2, m, 1) + at_high(2, halo_x(name, 0, c, z, 1), 1)
                    ref[FACE][dim, c, z] = step * (m + high)
            step = 0.25 * halo_y(FIRST, 1, 3, z) * (halo_y(name, 1, 3, z) - p[0:1])
            for c in range(3):
                ref[FACE_LOW, 1][c, z : z + 1, :] = step * (
                    halo_y(name, 1, c, z) + saved[c, z, 0:1, :]
                )
            step = 0.25 * halo_x(FIRST, 1, 3, z, 1) * (halo_x(name, 1, 3, z, 1) - p)
            for c in range(3):
                ref[FACE_LOW, 2][c, z] = step * (halo_x(name, 1, c, z, 1) + saved[c, z])
        step = 0.25 * halo_z(FIRST, 1, 3) * (halo_z(name, 1, 3) - pressure[0])
        for c in range(3):
            ref[FACE_LOW, 0][c] = step * (halo_z(name, 1, c) + saved[c, 0])

    loads[SOURCE].wait()
    loads[ACTIVE].wait()
    loads[INVERSES].wait()
    for z in range(NZ):
        mask = ref[LOADED, ACTIVE][z].astype(jnp.float32)
        values = [ref[LOADED, SOURCE][c, z] * mask for c in range(3)]
        for c in range(3):
            rhs[c, z] = values[c]
        for c, value in enumerate(smoothed(values, z)):
            iterate[c, z] = value
    loads[TRANS].wait()
    pl.semaphore_wait(barrier, len(PEERS))

    for name, channels in ((FIRST, 3), (SECOND, 3), (THIRD, 1)):
        send_iterate(name, channels)
        if name == FIRST:
            loads[BLOCKS].wait()
        system_inside(channels)
        if name == FIRST:
            trans_sum_inside()
            loads[TWO].wait()
            loads[THREE].wait()
            pack_own_coef()
            spread_to_peers(OWN_COEF, ALL_COEF, COEF_SEM, range(0, len(PEERS), 4))
            loads[ONE].wait()
            spread_level(1)
            scales(1)
        elif name == SECOND:
            spread_to_peers(OWN_COEF, ALL_COEF, COEF_SEM, range(1, len(PEERS), 4))
            loads[FINE].wait()
            scales(0)
            send_level(RIMS, 1)
        else:
            spread_to_peers(OWN_COEF, ALL_COEF, COEF_SEM, range(2, len(PEERS), 4))
            loads[MOBILITIES].wait()
            loads[PRESSURE].wait()
            send_saved()
        receive(name)
        if name == FIRST:
            trans_sum_rims()
        for z in range(NZ):
            if name == THIRD:
                value = rhs[0, z] - system_row(name, 0, z)
                ref[B, 0][z] = value
                ref[X, 0][z] = ref[SCALE, 0][z] * value
            else:
                left = [rhs[c, z] - system_row(name, c, z) for c in range(3)]
                for c, value in enumerate(smoothed(left, z)):
                    iterate[c, z] = iterate[c, z] + value

    send_level(DOWN0, 0)
    residual_inside(0)
    spread_to_peers(OWN_COEF, ALL_COEF, COEF_SEM, range(3, len(PEERS), 4))
    receive(DOWN0)
    for z in range(4):
        pair = residual(DOWN0, 0, 2 * z) + residual(DOWN0, 0, 2 * z + 1)
        value = paired(pair, 1)
        ref[B, 1][z] = value
        ref[X, 1][z] = ref[SCALE, 1][z] * value

    send_level(DOWN1, 1)
    residual_inside(1)
    receive_from_peers(COEF_SEM)
    wide_coefs(2)
    receive(DOWN1)
    pack_own_b(
        [
            paired(residual(DOWN1, 1, 2 * z) + residual(DOWN1, 1, 2 * z + 1), 2)
            for z in range(2)
        ]
    )

    spread_to_peers(OWN_B, ALL_B, B_SEM, range(len(PEERS)))
    for level, planes in ((2, 8), (3, 4)):
        for z in (0, planes + 1):
            ref[WIDE_X, level][z] = jnp.zeros(WIDE, jnp.float32)
    wide_coefs(3)
    face_weights()
    receive(RIMS)
    receive_from_peers(B_SEM)
    wide_solve()

    corrections = [onto_fine(2 * me[0] + z) for z in range(4)]
    for z in range(4):
        ref[X, 1][z] = ref[X, 1][z] + corrections[1 + z // 2][0]
    residual_inside(1)
    for z in range(4):
        _, low_y, high_y, low_x, high_x = corrections[1 + z // 2]
        acc = residual(DOWN1, 1, z)
        if z == 0:
            acc = acc - halo_z(RIMS, 1, 0) * corrections[0][0]
        if z == 3:
            acc = acc - halo_z(RIMS, 0, 0) * corrections[3][0]
        acc = acc - at_low(1, halo_y(RIMS, 1, 0, z) * low_y, 2)
        acc = acc - at_high(1, halo_y(RIMS, 0, 0, z) * high_y, 2)
        acc = acc - at_low(2, halo_x(RIMS, 1, 0, z, 2) * low_x, 2)
        acc = acc - at_high(2, halo_x(RIMS, 0, 0, z, 2) * high_x, 2)
        ref[R, 1][z] = acc
    for z in range(4):
        ref[X, 1][z] = ref[X, 1][z] + ref[SCALE, 1][z] * ref[R, 1][z]

    for z in range(NZ):
        ref[X, 0][z] = ref[X, 0][z] + ref[X, 1][z // 2]
    send_level(UP0, 0)
    residual_inside(0)
    receive(UP0)
    for z in range(NZ):
        ref[X, 0][z] = ref[X, 0][z] + ref[SCALE, 0][z] * residual(UP0, 0, z)

    loads[WEIGHTS].wait()
    name = LAST
    for z in range(NZ):
        mask = ref[LOADED, ACTIVE][z].astype(jnp.float32)
        for c in range(3):
            adjoint_ref[c, z] = mask * (iterate[c, z] + ref[LOADED, WEIGHTS][c, z] * ref[X, 0][z])
    for c in range(3):
        ref[SEND, name, 0, 1][c] = adjoint_ref[c, NZ - 1]
        ref[SEND, name, 0, 0][c] = adjoint_ref[c, 0]
    send(name, 0)
    for z in range(NZ):
        for c in range(3):
            ref[SEND, name, 1, 1][c, z : z + 1, :] = adjoint_ref[c, z, NY - 1 : NY, :]
            ref[SEND, name, 1, 0][c, z : z + 1, :] = adjoint_ref[c, z, 0:1, :]
    send(name, 1)
    high, low = zero, zero
    for z in range(NZ):
        for c in range(3):
            high = packed(high, adjoint_ref[c, z], 1, c, z, 1)
            low = packed(low, adjoint_ref[c, z], 0, c, z, 1)
    ref[SEND, name, 2, 1][...] = high
    ref[SEND, name, 2, 0][...] = low
    send(name, 2)

    face = ref[FACE]
    for dim in range(3):
        previous = None
        for z in range(NZ):
            flux = None
            for c in range(3):
                value = adjoint_ref[c, z]
                if dim == 0:
                    drop = value - adjoint_ref[c, z + 1] if z < NZ - 1 else value
                else:
                    drop = value - from_high(dim, value, 1)
                term = face[dim, c, z] * drop
                flux = term if flux is None else flux + term
            if dim == 0:
                gradient_ref[dim, z] = flux if previous is None else flux + previous
                previous = flux
            else:
                gradient_ref[dim, z] = flux + from_low(dim, flux, 1)
    receive(name)
    low_z, high_z = zero, zero
    for c in range(3):
        low_z = low_z + ref[FACE_LOW, 0][c] * (halo_z(name, 1, c) - adjoint_ref[c, 0])
        high_z = high_z + face[0, c, NZ - 1] * halo_z(name, 0, c)
    gradient_ref[0, 0] = gradient_ref[0, 0] + low_z
    gradient_ref[0, NZ - 1] = gradient_ref[0, NZ - 1] - high_z
    for z in range(NZ):
        low_y, high_y, low_x, high_x = zero, zero, zero, zero
        for c in range(3):
            value = adjoint_ref[c, z]
            low_y = low_y + ref[FACE_LOW, 1][c, z : z + 1, :] * (halo_y(name, 1, c, z) - value)
            high_y = high_y + face[1, c, z] * halo_y(name, 0, c, z)
            low_x = low_x + ref[FACE_LOW, 2][c, z] * (halo_x(name, 1, c, z, 1) - value)
            high_x = high_x + face[2, c, z] * halo_x(name, 0, c, z, 1)
        gradient_ref[1, z] = gradient_ref[1, z] + at_low(1, low_y, 1) - at_high(1, high_y, 1)
        gradient_ref[2, z] = gradient_ref[2, z] + at_low(2, low_x, 1) - at_high(2, high_x, 1)

    for copy in copies:
        copy.wait_send()


def solution(mesh):
    sizes = [mesh.shape[axis] for axis in AXES]

    def local(*args):
        table = scratch_table([(arg.shape, arg.dtype) for arg in args])
        out = jax.ShapeDtypeStruct((3, NZ) + PLANE, jnp.float32)
        return pl.pallas_call(
            functools.partial(kernel, sizes, tuple(table)),
            out_shape=(out, out),
            in_specs=[pl.BlockSpec(memory_space=pl.ANY)] * len(args),
            out_specs=(pl.BlockSpec(memory_space=pltpu.VMEM),) * 2,
            scratch_shapes=list(table.values()),
            compiler_params=pltpu.CompilerParams(collective_id=0, has_side_effects=True),
        )(*args)

    field = P("layer", "gy", "gx")
    stacked = P(None, "layer", "gy", "gx")
    return jax.shard_map(
        local,
        mesh=mesh,
        in_specs=(stacked, field) + (stacked,) * 8 + (field, stacked),
        out_specs=(stacked, stacked),
        check_vma=False,
    )
```

```python
import functools

import jax
import jax.numpy as jnp
from jax import lax
from jax.experimental import pallas as pl
from jax.experimental.pallas import tpu as pltpu
from jax.sharding import PartitionSpec as P

MESH = pl.DeviceIdType.MESH
OMEGA = 0.8
COARSE_SWEEPS = 4
AXES = ("layer", "gy", "gx")
NZ, NY, NX = 8, 16, 128
PLANE = (NY, NX)

FIRST, SECOND, THIRD, SAVED, RIMS, DOWN0, DOWN1, UP0, LAST = range(9)
ROUNDS = (
    (4, 3, 8),
    (3, 3, 8),
    (1, 1, 8),
    (4, 4, 8),
    (1, 1, 4),
    (1, 1, 8),
    (1, 1, 4),
    (1, 1, 8),
    (3, 3, 8),
)

(SOURCE, ACTIVE, BLOCKS, INVERSES, TRANS, WEIGHTS, FINE, ONE, TWO, THREE, PRESSURE, MOBILITIES) = range(12)
LOAD_ORDER = (SOURCE, ACTIVE, INVERSES, TRANS, BLOCKS, TWO, THREE, ONE, FINE, MOBILITIES, PRESSURE, WEIGHTS)

(
    LOADED,
    SEND,
    RECV,
    RHS,
    ITERATE,
    TOTAL,
    TRANS_SUM,
    COEF,
    SCALE,
    B,
    X,
    R,
    FACE,
    FACE_LOW,
    OWN_COEF,
    ALL_COEF,
    OWN_B,
    ALL_B,
    WIDE_COEF,
    WIDE_SCALE,
    WIDE_B,
    WIDE_X,
    WIDE_R,
    LOAD_SEM,
    SEND_SEM,
    RECV_SEM,
    COEF_SEM,
    B_SEM,
    ADJOINT,
    GRADIENT,
    OUT_SEM,
) = range(31)

WIDE = (32, 128)
REACH_Y = 3
PEERS = tuple(
    (a, b, c)
    for b in range(-REACH_Y, REACH_Y + 1)
    for a in (-1, 0, 1)
    for c in range(4)
    if (a, b, c) != (0, 0, 0)
    and (abs(b) < 3 or (a == 0 and c == 0))
    and (abs(b) < 2 or a == 0 or c != 2)
)


def message_shape(name, dim, up):
    fields_up, fields_down, planes = ROUNDS[name]
    fields = fields_up if up else fields_down
    if dim == 0:
        return (fields, NY, NX)
    if dim == 1:
        return (fields, planes, NX)
    return PLANE


def scratch_table(shapes):
    def vmem(*shape):
        return pltpu.VMEM(shape, jnp.float32)

    table = {}
    for name, (shape, dtype) in enumerate(shapes):
        table[LOADED, name] = pltpu.VMEM(shape, dtype)
    for name in (RHS, ITERATE, TOTAL, ADJOINT, GRADIENT):
        table[name] = vmem(3, NZ, *PLANE)
    table[TRANS_SUM] = vmem(NZ, *PLANE)
    for level in (0, 1):
        planes = NZ >> level
        if level:
            table[COEF, level] = vmem(7, planes, *PLANE)
        for name in (SCALE, B, X, R):
            table[name, level] = vmem(planes, *PLANE)
    table[FACE] = vmem(3, 3, NZ, *PLANE)
    table[FACE_LOW, 0] = vmem(3, *PLANE)
    table[FACE_LOW, 1] = vmem(3, NZ, NX)
    table[FACE_LOW, 2] = vmem(3, NZ, *PLANE)
    table[OWN_COEF] = vmem(16, NX)
    table[ALL_COEF] = vmem(3, 4, 2 * REACH_Y + 1, 16, NX)
    table[OWN_B] = vmem(2, NX)
    table[ALL_B] = vmem(3, 4, 2 * REACH_Y + 1, 2, NX)
    for level in (2, 3):
        planes = 16 >> (level - 1)
        table[WIDE_COEF, level] = vmem(7, planes, *WIDE)
        for name in (WIDE_SCALE, WIDE_B, WIDE_R):
            table[name, level] = vmem(planes, *WIDE)
        table[WIDE_X, level] = vmem(planes + 2, *WIDE)
    for name in range(len(ROUNDS)):
        for dim in range(3):
            for up in (0, 1):
                table[SEND, name, dim, up] = vmem(*message_shape(name, dim, up))
                table[RECV, name, dim, up] = vmem(*message_shape(name, dim, up))
    table[OUT_SEM] = pltpu.SemaphoreType.DMA((4,))
    table[LOAD_SEM] = pltpu.SemaphoreType.DMA((len(shapes),))
    for name, count in ((SEND_SEM, 6 * len(ROUNDS)), (RECV_SEM, 6 * len(ROUNDS))):
        table[name] = pltpu.SemaphoreType.DMA((count,))
    for name in (COEF_SEM, B_SEM):
        table[name] = pltpu.SemaphoreType.DMA((2, len(PEERS)))
    return table


def rolled(value, amount, axis):
    amount = amount % value.shape[axis]
    return pltpu.roll(value, amount, axis) if amount else value


def kernel(sizes, scratch_names, *refs):
    hbm = refs[:12]
    adjoint_out, gradient_out = refs[12:14]
    ref = dict(zip(scratch_names, refs[14:]))
    adjoint_ref, gradient_ref = ref[ADJOINT], ref[GRADIENT]

    me = [lax.axis_index(axis) for axis in AXES]
    above = [lax.rem(me[d] + 1, sizes[d]) for d in range(3)]
    below = [lax.rem(me[d] + sizes[d] - 1, sizes[d]) for d in range(3)]

    loads = {}
    for name in LOAD_ORDER:
        loads[name] = pltpu.make_async_copy(
            hbm[name], ref[LOADED, name], ref[LOAD_SEM].at[name]
        )
        loads[name].start()

    for dx in range(3):
        for layer in range(4):
            for dy in range(2 * REACH_Y + 1):
                ref[ALL_COEF][dx, layer, dy] = jnp.zeros((16, NX), jnp.float32)
                ref[ALL_B][dx, layer, dy] = jnp.zeros((2, NX), jnp.float32)

    peer_x = {a: lax.rem(me[2] + (a + sizes[2]), sizes[2]) for a in (-1, 1)} | {0: me[2]}
    peer_y = {b: lax.rem(me[1] + (b + sizes[1]), sizes[1]) for b in range(-REACH_Y, REACH_Y + 1)}
    peer_z = {c: lax.rem(me[0] + c, sizes[0]) for c in range(1, 4)} | {0: me[0]}
    peer_y[0] = me[1]

    def peer_of(offset):
        a, b, c = offset
        return (peer_x[a], peer_y[b], peer_z[c])

    barrier = pltpu.get_barrier_semaphore()
    for d in range(3):
        for peer in (above[d], below[d]):
            pl.semaphore_signal(barrier, inc=1, device_id={AXES[d]: peer}, device_id_type=MESH)

    low_on = [jnp.where(me[d] > 0, 1.0, 0.0).astype(jnp.float32) for d in range(3)]
    high_on = [jnp.where(me[d] < sizes[d] - 1, 1.0, 0.0).astype(jnp.float32) for d in range(3)]

    row = lax.broadcasted_iota(jnp.int32, PLANE, 0)
    lane = lax.broadcasted_iota(jnp.int32, PLANE, 1)
    zero = jnp.zeros(PLANE, jnp.float32)
    copies = []
    arrivals = {}

    def send(name, dim):
        for up in (1, 0):
            k = name * 6 + dim * 2 + up
            copy = pltpu.make_async_remote_copy(
                src_ref=ref[SEND, name, dim, up],
                dst_ref=ref[RECV, name, dim, up],
                send_sem=ref[SEND_SEM].at[k],
                recv_sem=ref[RECV_SEM].at[k],
                device_id={AXES[dim]: above[dim] if up else below[dim]},
                device_id_type=MESH,
            )
            copy.start()
            copies.append(copy)
            arrivals[name, dim, up] = copy

    def receive(name):
        for dim in range(3):
            for up in (1, 0):
                arrivals[name, dim, up].wait_recv()

    def offset(field, z, stride):
        return field * NZ + z * stride

    def packed(current, value, up, field, z, stride):
        at = offset(field, z, stride)
        moved = rolled(value, at + stride if up else at, 1)
        return jnp.where((lane >= at) & (lane < at + stride), moved, current)

    def halo_y(name, up, field, z):
        on = low_on[1] if up else high_on[1]
        return ref[RECV, name, 1, up][field, z : z + 1, :] * on

    def halo_x(name, up, field, z, stride):
        at = offset(field, z, stride)
        pack = ref[RECV, name, 2, up][...] * (low_on[2] if up else high_on[2])
        return rolled(pack, NX - at if up else 2 * NX - stride - at, 1)

    def halo_z(name, up, field):
        return ref[RECV, name, 0, up][field] * (low_on[0] if up else high_on[0])

    def at_low(dim, value, stride):
        return jnp.where((row if dim == 1 else lane) < stride, value, 0.0)

    def at_high(dim, value, stride):
        return jnp.where((row if dim == 1 else lane) >= PLANE[dim - 1] - stride, value, 0.0)

    def from_low(dim, value, stride):
        return jnp.where(
            (row if dim == 1 else lane) < stride, 0.0, rolled(value, stride, dim - 1)
        )

    def from_high(dim, value, stride):
        size = PLANE[dim - 1]
        return jnp.where(
            (row if dim == 1 else lane) >= size - stride, 0.0, rolled(value, -stride, dim - 1)
        )

    trans, blocks, inverses = ref[LOADED, TRANS], ref[LOADED, BLOCKS], ref[LOADED, INVERSES]
    iterate, rhs, total = ref[ITERATE], ref[RHS], ref[TOTAL]

    def smoothed(residual, z):
        return [
            inverses[c, z] * residual[0]
            + inverses[3 + c, z] * residual[1]
            + inverses[6 + c, z] * residual[2]
            for c in range(3)
        ]

    def send_iterate(name, channels):
        first = name == FIRST
        for c in range(channels):
            ref[SEND, name, 0, 1][c] = trans[0, NZ - 1] * iterate[c, NZ - 1]
            ref[SEND, name, 0, 0][c] = iterate[c, 0]
        if first:
            ref[SEND, name, 0, 1][channels] = trans[0, NZ - 1]
        send(name, 0)
        for z in range(NZ):
            coef = trans[1, z, NY - 1 : NY, :]
            for c in range(channels):
                ref[SEND, name, 1, 1][c, z : z + 1, :] = coef * iterate[c, z, NY - 1 : NY, :]
                ref[SEND, name, 1, 0][c, z : z + 1, :] = iterate[c, z, 0:1, :]
            if first:
                ref[SEND, name, 1, 1][channels, z : z + 1, :] = coef
        send(name, 1)
        high, low = zero, zero
        for z in range(NZ):
            coef = trans[2, z]
            for c in range(channels):
                high = packed(high, coef * iterate[c, z], 1, c, z, 1)
                low = packed(low, iterate[c, z], 0, c, z, 1)
            if first:
                high = packed(high, coef, 1, channels, z, 1)
        ref[SEND, name, 2, 1][...] = high
        ref[SEND, name, 2, 0][...] = low
        send(name, 2)

    def system_inside(channels):
        for z in range(NZ):
            values = [iterate[c, z] for c in range(3)]
            for c in range(channels):
                value = values[c]
                acc = (
                    blocks[c, z] * values[0]
                    + blocks[3 + c, z] * values[1]
                    + blocks[6 + c, z] * values[2]
                )
                if z > 0:
                    acc = acc - trans[0, z - 1] * iterate[c, z - 1]
                if z < NZ - 1:
                    acc = acc - trans[0, z] * iterate[c, z + 1]
                for dim in (1, 2):
                    coef = trans[dim, z]
                    acc = acc - from_low(dim, coef * value, 1)
                    acc = acc - coef * from_high(dim, value, 1)
                total[c, z] = acc

    def system_row(name, c, z):
        acc = total[c, z] + ref[TRANS_SUM][z] * iterate[c, z]
        if z == 0:
            acc = acc - halo_z(name, 1, c)
        if z == NZ - 1:
            acc = acc - trans[0, z] * halo_z(name, 0, c)
        acc = acc - at_low(1, halo_y(name, 1, c, z), 1)
        acc = acc - at_high(1, trans[1, z] * halo_y(name, 0, c, z), 1)
        acc = acc - at_low(2, halo_x(name, 1, c, z, 1), 1)
        acc = acc - at_high(2, trans[2, z] * halo_x(name, 0, c, z, 1), 1)
        return acc

    def trans_sum_inside():
        for z in range(NZ):
            acc = trans[0, z] + trans[1, z] + trans[2, z]
            if z > 0:
                acc = acc + trans[0, z - 1]
            for dim in (1, 2):
                acc = acc + from_low(dim, trans[dim, z], 1)
            ref[TRANS_SUM][z] = acc

    def trans_sum_rims():
        for z in range(NZ):
            acc = ref[TRANS_SUM][z]
            if z == 0:
                acc = acc + halo_z(FIRST, 1, 3)
            acc = acc + at_low(1, halo_y(FIRST, 1, 3, z), 1)
            acc = acc + at_low(2, halo_x(FIRST, 1, 3, z, 1), 1)
            ref[TRANS_SUM][z] = acc

    def coef(level, k, z):
        return ref[LOADED, FINE][k, z] if level == 0 else ref[COEF, level][k, z]

    def spread_level(level):
        rows, lanes = NY >> level, NX >> level
        source = ref[LOADED, ONE]
        pick = lax.broadcasted_iota(jnp.int32, (8, NX), 1) // (1 << level)
        for z in range(NZ >> level):
            for k in range(7):
                value = source[k, z]
                value = jnp.concatenate([value] * (1 << level), axis=1)
                if rows < 8:
                    value = jnp.concatenate([value] * (8 // rows), axis=0)
                value = jnp.take_along_axis(value, pick, axis=1, mode="promise_in_bounds")
                wide = jnp.broadcast_to(value[0:1], PLANE)
                for y in range(1, rows):
                    wide = jnp.where(row < y << level, wide, jnp.broadcast_to(value[y : y + 1], PLANE))
                ref[COEF, level][k, z] = wide

    def scales(level):
        for z in range(NZ >> level):
            ref[SCALE, level][z] = OMEGA / coef(level, 0, z)

    def send_level(name, level):
        planes, stride = NZ >> level, 1 << level
        x = [1.0] * planes if name == RIMS else ref[X, level]
        ref[SEND, name, 0, 1][0] = coef(level, 2, planes - 1) * x[planes - 1]
        ref[SEND, name, 0, 0][0] = coef(level, 1, 0) * x[0]
        send(name, 0)
        for z in range(planes):
            ref[SEND, name, 1, 1][0, z : z + 1, :] = (coef(level, 4, z) * x[z])[NY - 1 : NY]
            ref[SEND, name, 1, 0][0, z : z + 1, :] = (coef(level, 3, z) * x[z])[0:1]
        send(name, 1)
        high, low = zero, zero
        for z in range(planes):
            high = packed(high, coef(level, 6, z) * x[z], 1, 0, z, stride)
            low = packed(low, coef(level, 5, z) * x[z], 0, 0, z, stride)
        ref[SEND, name, 2, 1][...] = high
        ref[SEND, name, 2, 0][...] = low
        send(name, 2)

    def residual_inside(level):
        planes, stride = NZ >> level, 1 << level
        x, b, r = ref[X, level], ref[B, level], ref[R, level]
        for z in range(planes):
            acc = b[z] - coef(level, 0, z) * x[z]
            if z > 0:
                acc = acc - coef(level, 2, z - 1) * x[z - 1]
            if z < planes - 1:
                acc = acc - coef(level, 1, z + 1) * x[z + 1]
            for dim in (1, 2):
                acc = acc - from_low(dim, coef(level, 2 * dim + 2, z) * x[z], stride)
                acc = acc - from_high(dim, coef(level, 2 * dim + 1, z) * x[z], stride)
            r[z] = acc

    def residual(name, level, z):
        planes, stride = NZ >> level, 1 << level
        acc = ref[R, level][z]
        if z == 0:
            acc = acc - halo_z(name, 1, 0)
        if z == planes - 1:
            acc = acc - halo_z(name, 0, 0)
        acc = acc - at_low(1, halo_y(name, 1, 0, z), stride)
        acc = acc - at_high(1, halo_y(name, 0, 0, z), stride)
        acc = acc - at_low(2, halo_x(name, 1, 0, z, stride), stride)
        acc = acc - at_high(2, halo_x(name, 0, 0, z, stride), stride)
        return acc

    def paired(value, stride):
        for dim, place in ((0, row), (1, lane)):
            upper = (place & stride) != 0
            value = value + jnp.where(
                upper, rolled(value, stride, dim), rolled(value, -stride, dim)
            )
        return value

    row8 = lax.broadcasted_iota(jnp.int32, (8, NX), 0)
    lane8 = lax.broadcasted_iota(jnp.int32, (8, NX), 1)
    lane1 = lax.broadcasted_iota(jnp.int32, (1, NX), 1)
    windows = 2 * REACH_Y + 1

    def along_lanes(value, index):
        return jnp.take_along_axis(value, index, axis=1, mode="promise_in_bounds")

    def pack_own_coef():
        for k in range(7):
            place = lax.broadcasted_iota(jnp.int32, (4, NX), 0)
            lanes = lax.broadcasted_iota(jnp.int32, (4, NX), 1)
            for z in range(2):
                value = jnp.concatenate([ref[LOADED, TWO][k, z]] * 4, axis=1)
                value = jnp.where(lanes // 32 == place, value, 0.0)
                at = 2 * k + z
                ref[OWN_COEF][at : at + 1, :] = jnp.sum(value, axis=0, keepdims=True)
        place = lax.broadcasted_iota(jnp.int32, (2, NX), 0)
        lanes = lax.broadcasted_iota(jnp.int32, (2, NX), 1)
        for half in range(2):
            packed_row = jnp.zeros((1, NX), jnp.float32)
            for k in range(4 * half, min(7, 4 * half + 4)):
                value = jnp.concatenate([ref[LOADED, THREE][k, 0]] * 8, axis=1)
                value = jnp.where((lanes % 32) // 16 == place, value, 0.0)
                value = jnp.sum(value, axis=0, keepdims=True)
                packed_row = jnp.where(lane1 // 32 == k % 4, value, packed_row)
            ref[OWN_COEF][14 + half : 15 + half, :] = packed_row
        ref[ALL_COEF][1, me[0], REACH_Y] = ref[OWN_COEF][...]

    def pack_own_b(planes):
        for z, plane in enumerate(planes):
            total_row = jnp.zeros((8, NX), jnp.float32)
            for half in range(2):
                value = along_lanes(plane[8 * half : 8 * half + 8], 4 * (lane8 % 32))
                keep = (row8 % 4 == 0) & (row8 // 4 + 2 * half == lane8 // 32)
                total_row = total_row + jnp.where(keep, value, 0.0)
            ref[OWN_B][z : z + 1, :] = jnp.sum(total_row, axis=0, keepdims=True)
        ref[ALL_B][1, me[0], REACH_Y] = ref[OWN_B][...]

    def spread_to_peers(own, everyone, sems, chosen):
        for i in chosen:
            a, b, c = PEERS[i]
            copy = pltpu.make_async_remote_copy(
                src_ref=ref[own],
                dst_ref=ref[everyone].at[1 - a, me[0], REACH_Y - b],
                send_sem=ref[sems].at[0, i],
                recv_sem=ref[sems].at[1, i],
                device_id=peer_of(PEERS[i]),
                device_id_type=MESH,
            )
            copy.start()
            copies.append(copy)
            arrivals[sems, i] = copy

    def steps_away(steps):
        return [i for i, (a, b, c) in enumerate(PEERS) if abs(a) + abs(b) + min(c, 4 - c) == steps]

    def receive_from_peers(sems):
        for i in range(len(PEERS)):
            arrivals[sems, i].wait_recv()

    def inside(value, size):
        return jnp.where((value >= 0) & (value < size), 1.0, 0.0).astype(jnp.float32)

    in_y = [inside(me[1] + (dy - REACH_Y), sizes[1]) for dy in range(windows)]
    in_x = [inside(me[2] + (dx - 1), sizes[2]) for dx in range(3)]

    def unpacked(everyone, layer, at, level, base, masked):
        width, rows = (32, row8 % 4) if level == 2 else (16, row8 % 4 // 2)
        step = 2 if level == 2 else 4
        start = base + rows * width
        middle = start + (lane8 - 32) // step
        sides = start + jnp.where(lane8 < 32, width // 2 + lane8 // step, (lane8 - 96) // step)
        tiles = []
        for t in range(4):
            halves = []
            for dy in (2 * t, 2 * t + 1):
                if dy >= windows:
                    blank = jnp.zeros((1, NX), jnp.float32)
                    halves.append((blank, blank))
                    continue
                left, own, right = [
                    ref[everyone][dx, layer, dy, at : at + 1, :] for dx in range(3)
                ]
                if masked:
                    left, own, right = (
                        left * (in_x[0] * in_y[dy]),
                        own * in_y[dy],
                        right * (in_x[2] * in_y[dy]),
                    )
                halves.append((own, jnp.where(lane1 % width < width // 2, right, left)))
            own, both = [
                jnp.where(
                    row8 < 4,
                    jnp.broadcast_to(halves[0][i], (8, NX)),
                    jnp.broadcast_to(halves[1][i], (8, NX)),
                )
                for i in range(2)
            ]
            tiles.append(
                jnp.where(
                    (lane8 >= 32) & (lane8 < 96),
                    along_lanes(own, jnp.clip(middle, 0, NX - 1)),
                    along_lanes(both, sides),
                )
            )
        return tiles

    def wide_coefs(level):
        for layer in range(4):
            for k in range(7):
                for zz in range(2 if level == 2 else 1):
                    at, base = (2 * k + zz, 0) if level == 2 else (14 + k // 4, k % 4 * 32)
                    plane = 2 * layer + zz if level == 2 else layer
                    for t, tile in enumerate(unpacked(ALL_COEF, layer, at, level, base, True)):
                        ref[WIDE_COEF, level][k, plane, 8 * t : 8 * t + 8, :] = tile
                        if k == 0:
                            live = tile > 0.0
                            ref[WIDE_SCALE, level][plane, 8 * t : 8 * t + 8, :] = jnp.where(
                                live, OMEGA / jnp.where(live, tile, 1.0), 0.0
                            )

    def wide_residual(level, z):
        planes = 16 >> (level - 1)
        rows, lanes = (1, 2) if level == 2 else (2, 4)
        a, x = ref[WIDE_COEF, level], ref[WIDE_X, level]
        acc = ref[WIDE_B, level][z] - a[0, z] * x[z + 1]
        if z > 0:
            acc = acc - a[2, z - 1] * x[z]
        if z < planes - 1:
            acc = acc - a[1, z + 1] * x[z + 2]
        for dim, stride in ((0, rows), (1, lanes)):
            acc = acc - rolled(a[2 * dim + 4, z] * x[z + 1], stride, dim)
            acc = acc - rolled(a[2 * dim + 3, z] * x[z + 1], -stride, dim)
        return acc

    def wide_relax(level):
        planes = 16 >> (level - 1)
        for z in range(planes):
            ref[WIDE_R, level][z] = wide_residual(level, z)
        x = ref[WIDE_X, level]
        for z in range(planes):
            x[z + 1] = x[z + 1] + ref[WIDE_SCALE, level][z] * ref[WIDE_R, level][z]

    def wide_start(level, z, value):
        ref[WIDE_B, level][z] = value
        ref[WIDE_X, level][z + 1] = ref[WIDE_SCALE, level][z] * value

    def wide_solve():
        wide_row = lax.broadcasted_iota(jnp.int32, WIDE, 0)
        wide_lane = lax.broadcasted_iota(jnp.int32, WIDE, 1)
        for layer in range(4):
            for zz in range(2):
                tiles = unpacked(ALL_B, layer, zz, 2, 0, False)
                wide_start(2, 2 * layer + zz, jnp.concatenate(tiles, axis=0))
        for z in range(4):
            pair = wide_residual(2, 2 * z) + wide_residual(2, 2 * z + 1)
            for dim, place, stride in ((0, wide_row, 1), (1, wide_lane, 2)):
                upper = (place & stride) != 0
                pair = pair + jnp.where(
                    upper, rolled(pair, stride, dim), rolled(pair, -stride, dim)
                )
            wide_start(3, z, pair)
        for sweep in range(COARSE_SWEEPS - 1):
            wide_relax(3)
        for z in range(8):
            ref[WIDE_X, 2][z + 1] = ref[WIDE_X, 2][z + 1] + ref[WIDE_X, 3][z // 2 + 1]
        wide_relax(2)

    def onto_fine(wide_plane):
        x = ref[WIDE_X, 2]
        tile = x[wide_plane, 8:16, :]
        after = x[wide_plane, 16:24, :]
        here = 32 + lane8 // 4 * 2

        def rows_of(value):
            wide = jnp.broadcast_to(value[4:5], PLANE)
            for y in range(1, 4):
                wide = jnp.where(row < 4 * y, wide, jnp.broadcast_to(value[4 + y : 5 + y], PLANE))
            return wide

        own = along_lanes(tile, here)
        return (
            rows_of(own),
            own[3:4],
            along_lanes(after, here)[0:1],
            rows_of(along_lanes(tile, 31 + 0 * lane8)),
            rows_of(along_lanes(tile, 96 + 0 * lane8)),
        )

    saved, pressure = ref[LOADED, MOBILITIES], ref[LOADED, PRESSURE]

    def send_saved():
        name = SAVED
        fields = [lambda z, c=c: saved[c, z] for c in range(3)] + [lambda z: pressure[z]]
        for f, field in enumerate(fields):
            ref[SEND, name, 0, 1][f] = field(NZ - 1)
            ref[SEND, name, 0, 0][f] = field(0)
        send(name, 0)
        for f, field in enumerate(fields):
            for z in range(NZ):
                ref[SEND, name, 1, 1][f, z : z + 1, :] = field(z)[NY - 1 : NY]
                ref[SEND, name, 1, 0][f, z : z + 1, :] = field(z)[0:1]
        send(name, 1)
        high, low = zero, zero
        for f, field in enumerate(fields):
            for z in range(NZ):
                high = packed(high, field(z), 1, f, z, 1)
                low = packed(low, field(z), 0, f, z, 1)
        ref[SEND, name, 2, 1][...] = high
        ref[SEND, name, 2, 0][...] = low
        send(name, 2)

    def face_weights():
        name = SAVED
        receive(name)
        for z in range(NZ):
            p = pressure[z]
            for dim in range(3):
                if dim == 0:
                    high = pressure[z + 1] if z < NZ - 1 else halo_z(name, 0, 3)
                elif dim == 1:
                    high = from_high(1, p, 1) + at_high(1, halo_y(name, 0, 3, z), 1)
                else:
                    high = from_high(2, p, 1) + at_high(2, halo_x(name, 0, 3, z, 1), 1)
                step = 0.25 * trans[dim, z] * (p - high)
                for c in range(3):
                    m = saved[c, z]
                    if dim == 0:
                        high = saved[c, z + 1] if z < NZ - 1 else halo_z(name, 0, c)
                    elif dim == 1:
                        high = from_high(1, m, 1) + at_high(1, halo_y(name, 0, c, z), 1)
                    else:
                        high = from_high(2, m, 1) + at_high(2, halo_x(name, 0, c, z, 1), 1)
                    ref[FACE][dim, c, z] = step * (m + high)
            step = 0.25 * halo_y(FIRST, 1, 3, z) * (halo_y(name, 1, 3, z) - p[0:1])
            for c in range(3):
                ref[FACE_LOW, 1][c, z : z + 1, :] = step * (
                    halo_y(name, 1, c, z) + saved[c, z, 0:1, :]
                )
            step = 0.25 * halo_x(FIRST, 1, 3, z, 1) * (halo_x(name, 1, 3, z, 1) - p)
            for c in range(3):
                ref[FACE_LOW, 2][c, z] = step * (halo_x(name, 1, c, z, 1) + saved[c, z])
        step = 0.25 * halo_z(FIRST, 1, 3) * (halo_z(name, 1, 3) - pressure[0])
        for c in range(3):
            ref[FACE_LOW, 0][c] = step * (halo_z(name, 1, c) + saved[c, 0])

    loads[SOURCE].wait()
    loads[ACTIVE].wait()
    loads[INVERSES].wait()
    for z in range(NZ):
        mask = ref[LOADED, ACTIVE][z].astype(jnp.float32)
        values = [ref[LOADED, SOURCE][c, z] * mask for c in range(3)]
        for c in range(3):
            rhs[c, z] = values[c]
        for c, value in enumerate(smoothed(values, z)):
            iterate[c, z] = value
    loads[TRANS].wait()
    pl.semaphore_wait(barrier, 6)

    for name, channels in ((FIRST, 3), (SECOND, 3), (THIRD, 1)):
        send_iterate(name, channels)
        if name == FIRST:
            loads[BLOCKS].wait()
        system_inside(channels)
        if name == FIRST:
            trans_sum_inside()
            loads[TWO].wait()
            loads[THREE].wait()
            pack_own_coef()
            spread_to_peers(OWN_COEF, ALL_COEF, COEF_SEM, steps_away(1))
            loads[ONE].wait()
            spread_level(1)
            scales(1)
        elif name == SECOND:
            spread_to_peers(OWN_COEF, ALL_COEF, COEF_SEM, steps_away(2))
            loads[FINE].wait()
            scales(0)
            send_level(RIMS, 1)
        else:
            spread_to_peers(OWN_COEF, ALL_COEF, COEF_SEM, steps_away(3))
            loads[MOBILITIES].wait()
            loads[PRESSURE].wait()
            send_saved()
        receive(name)
        if name == FIRST:
            trans_sum_rims()
        for z in range(NZ):
            if name == THIRD:
                value = rhs[0, z] - system_row(name, 0, z)
                ref[B, 0][z] = value
                ref[X, 0][z] = ref[SCALE, 0][z] * value
            else:
                left = [rhs[c, z] - system_row(name, c, z) for c in range(3)]
                for c, value in enumerate(smoothed(left, z)):
                    iterate[c, z] = iterate[c, z] + value

    send_level(DOWN0, 0)
    residual_inside(0)
    spread_to_peers(OWN_COEF, ALL_COEF, COEF_SEM, steps_away(4))
    receive(DOWN0)
    for z in range(4):
        pair = residual(DOWN0, 0, 2 * z) + residual(DOWN0, 0, 2 * z + 1)
        value = paired(pair, 1)
        ref[B, 1][z] = value
        ref[X, 1][z] = ref[SCALE, 1][z] * value

    send_level(DOWN1, 1)
    residual_inside(1)
    receive_from_peers(COEF_SEM)
    wide_coefs(2)
    receive(DOWN1)
    pack_own_b(
        [
            paired(residual(DOWN1, 1, 2 * z) + residual(DOWN1, 1, 2 * z + 1), 2)
            for z in range(2)
        ]
    )

    spread_to_peers(OWN_B, ALL_B, B_SEM, range(len(PEERS)))
    for level, planes in ((2, 8), (3, 4)):
        for z in (0, planes + 1):
            ref[WIDE_X, level][z] = jnp.zeros(WIDE, jnp.float32)
    wide_coefs(3)
    face_weights()
    receive(RIMS)
    receive_from_peers(B_SEM)
    wide_solve()

    corrections = [onto_fine(2 * me[0] + z) for z in range(4)]
    for z in range(4):
        ref[X, 1][z] = ref[X, 1][z] + corrections[1 + z // 2][0]
    residual_inside(1)
    for z in range(4):
        _, low_y, high_y, low_x, high_x = corrections[1 + z // 2]
        acc = residual(DOWN1, 1, z)
        if z == 0:
            acc = acc - halo_z(RIMS, 1, 0) * corrections[0][0]
        if z == 3:
            acc = acc - halo_z(RIMS, 0, 0) * corrections[3][0]
        acc = acc - at_low(1, halo_y(RIMS, 1, 0, z) * low_y, 2)
        acc = acc - at_high(1, halo_y(RIMS, 0, 0, z) * high_y, 2)
        acc = acc - at_low(2, halo_x(RIMS, 1, 0, z, 2) * low_x, 2)
        acc = acc - at_high(2, halo_x(RIMS, 0, 0, z, 2) * high_x, 2)
        ref[R, 1][z] = acc
    for z in range(4):
        ref[X, 1][z] = ref[X, 1][z] + ref[SCALE, 1][z] * ref[R, 1][z]

    for z in range(NZ):
        ref[X, 0][z] = ref[X, 0][z] + ref[X, 1][z // 2]
    send_level(UP0, 0)
    residual_inside(0)
    receive(UP0)
    for z in range(NZ):
        ref[X, 0][z] = ref[X, 0][z] + ref[SCALE, 0][z] * residual(UP0, 0, z)

    loads[WEIGHTS].wait()
    name = LAST
    stores = [pltpu.make_async_copy(adjoint_ref, adjoint_out, ref[OUT_SEM].at[3])]
    for dim in range(3):
        stores.append(
            pltpu.make_async_copy(gradient_ref.at[dim], gradient_out.at[dim], ref[OUT_SEM].at[dim])
        )
    for z in range(NZ):
        mask = ref[LOADED, ACTIVE][z].astype(jnp.float32)
        for c in range(3):
            adjoint_ref[c, z] = mask * (iterate[c, z] + ref[LOADED, WEIGHTS][c, z] * ref[X, 0][z])
    for c in range(3):
        ref[SEND, name, 0, 1][c] = adjoint_ref[c, NZ - 1]
        ref[SEND, name, 0, 0][c] = adjoint_ref[c, 0]
    send(name, 0)
    for z in range(NZ):
        for c in range(3):
            ref[SEND, name, 1, 1][c, z : z + 1, :] = adjoint_ref[c, z, NY - 1 : NY, :]
            ref[SEND, name, 1, 0][c, z : z + 1, :] = adjoint_ref[c, z, 0:1, :]
    send(name, 1)
    high, low = zero, zero
    for z in range(NZ):
        for c in range(3):
            high = packed(high, adjoint_ref[c, z], 1, c, z, 1)
            low = packed(low, adjoint_ref[c, z], 0, c, z, 1)
    ref[SEND, name, 2, 1][...] = high
    ref[SEND, name, 2, 0][...] = low
    send(name, 2)

    stores[0].start()
    face = ref[FACE]
    for dim in range(3):
        previous = None
        for z in range(NZ):
            flux = None
            for c in range(3):
                value = adjoint_ref[c, z]
                if dim == 0:
                    drop = value - adjoint_ref[c, z + 1] if z < NZ - 1 else value
                else:
                    drop = value - from_high(dim, value, 1)
                term = face[dim, c, z] * drop
                flux = term if flux is None else flux + term
            if dim == 0:
                gradient_ref[dim, z] = flux if previous is None else flux + previous
                previous = flux
            else:
                gradient_ref[dim, z] = flux + from_low(dim, flux, 1)
    receive(name)
    low_z, high_z = zero, zero
    for c in range(3):
        low_z = low_z + ref[FACE_LOW, 0][c] * (halo_z(name, 1, c) - adjoint_ref[c, 0])
        high_z = high_z + face[0, c, NZ - 1] * halo_z(name, 0, c)
    gradient_ref[0, 0] = gradient_ref[0, 0] + low_z
    gradient_ref[0, NZ - 1] = gradient_ref[0, NZ - 1] - high_z
    stores[1].start()
    for dim, halo in ((1, lambda *at: halo_y(name, *at)), (2, lambda *at: halo_x(name, *at, 1))):
        for z in range(NZ):
            low, high = zero, zero
            for c in range(3):
                rim = ref[FACE_LOW, 1][c, z : z + 1, :] if dim == 1 else ref[FACE_LOW, 2][c, z]
                low = low + rim * (halo(1, c, z) - adjoint_ref[c, z])
                high = high + face[dim, c, z] * halo(0, c, z)
            gradient_ref[dim, z] = gradient_ref[dim, z] + at_low(dim, low, 1) - at_high(dim, high, 1)
        stores[1 + dim].start()
    for store in stores:
        store.wait()
    for copy in copies:
        copy.wait_send()


def hand_over(adjoint_in, gradient_in, adjoint_out, gradient_out, buffer, sems):
    arrays = ((adjoint_in, adjoint_out), (gradient_in, gradient_out))
    chunks = [(i, c) for i in range(2) for c in range(3)]
    loads = [
        pltpu.make_async_copy(arrays[i][0].at[c], buffer.at[i, c], sems.at[0, 3 * i + c])
        for i, c in chunks
    ]
    stores = [
        pltpu.make_async_copy(buffer.at[i, c], arrays[i][1].at[c], sems.at[1, 3 * i + c])
        for i, c in chunks
    ]
    for load in loads:
        load.start()
    for load, store in zip(loads, stores):
        load.wait()
        store.start()
    for store in stores:
        store.wait()


def solution(mesh):
    sizes = [mesh.shape[axis] for axis in AXES]

    def local(*args):
        table = scratch_table([(arg.shape, arg.dtype) for arg in args])
        out = jax.ShapeDtypeStruct((3, NZ) + PLANE, jnp.float32)
        results = pl.pallas_call(
            functools.partial(kernel, sizes, tuple(table)),
            out_shape=(out, out),
            in_specs=[pl.BlockSpec(memory_space=pl.ANY)] * len(args),
            out_specs=(pl.BlockSpec(memory_space=pl.ANY),) * 2,
            scratch_shapes=list(table.values()),
            compiler_params=pltpu.CompilerParams(collective_id=0, has_side_effects=True),
        )(*args)
        return pl.pallas_call(
            hand_over,
            out_shape=(out, out),
            in_specs=[pl.BlockSpec(memory_space=pl.ANY)] * 2,
            out_specs=(pl.BlockSpec(memory_space=pl.ANY),) * 2,
            scratch_shapes=[
                pltpu.VMEM((2, 3, NZ) + PLANE, jnp.float32),
                pltpu.SemaphoreType.DMA((2, 6)),
            ],
        )(*results)

    field = P("layer", "gy", "gx")
    stacked = P(None, "layer", "gy", "gx")
    return jax.shard_map(
        local,
        mesh=mesh,
        in_specs=(stacked, field) + (stacked,) * 8 + (field, stacked),
        out_specs=(stacked, stacked),
        check_vma=False,
    )
```

```python
import functools

import jax
import jax.numpy as jnp
from jax import lax
from jax.experimental import pallas as pl
from jax.experimental.pallas import tpu as pltpu
from jax.sharding import PartitionSpec as P

MESH = pl.DeviceIdType.MESH
OMEGA = 0.8
COARSE_SWEEPS = 4
AXES = ("layer", "gy", "gx")
NZ, NY, NX = 8, 16, 128
PLANE = (NY, NX)

FIRST, SECOND, THIRD, SAVED, RIMS, RIMS0, EDGES, DOWN0, DOWN1, MIDDLE, LAST = range(11)
ROUNDS = (
    (4, 3, 8),
    (3, 3, 8),
    (1, 1, 8),
    (4, 4, 8),
    (1, 1, 4),
    (1, 1, 8),
    (6, 6, 4),
    (1, 1, 8),
    (1, 1, 4),
    (1, 1, 4),
    (3, 3, 8),
)

(SOURCE, ACTIVE, BLOCKS, INVERSES, TRANS, WEIGHTS, FINE, ONE, TWO, THREE, PRESSURE, MOBILITIES) = range(12)
LOAD_ORDER = (SOURCE, ACTIVE, INVERSES, TRANS, BLOCKS, TWO, THREE, ONE, FINE, MOBILITIES, PRESSURE, WEIGHTS)

(
    LOADED,
    SEND,
    RECV,
    RHS,
    ITERATE,
    TOTAL,
    TRANS_SUM,
    COEF,
    SCALE,
    B,
    X,
    R,
    FACE,
    FACE_LOW,
    OWN_COEF,
    ALL_COEF,
    OWN_B,
    ALL_B,
    WIDE_COEF,
    WIDE_SCALE,
    WIDE_B,
    WIDE_X,
    WIDE_R,
    LOAD_SEM,
    SEND_SEM,
    RECV_SEM,
    COEF_SEM,
    B_SEM,
    ADJOINT,
    GRADIENT,
    OUT_SEM,
    EDGE,
    MID,
) = range(33)

WIDE = (32, 128)
REACH_Y = 3
PEERS = tuple(
    (a, b, c)
    for b in range(-REACH_Y, REACH_Y + 1)
    for a in (-1, 0, 1)
    for c in range(4)
    if (a, b, c) != (0, 0, 0)
    and (abs(b) < 3 or c != 2)
)


def message_shape(name, dim, up):
    fields_up, fields_down, planes = ROUNDS[name]
    fields = fields_up if up else fields_down
    if dim == 0:
        return (fields, NY, NX)
    if dim == 1:
        return (fields, planes, NX)
    return PLANE


def scratch_table(shapes):
    def vmem(*shape):
        return pltpu.VMEM(shape, jnp.float32)

    table = {}
    for name, (shape, dtype) in enumerate(shapes):
        table[LOADED, name] = pltpu.VMEM(shape, dtype)
    for name in (RHS, ITERATE, TOTAL, ADJOINT, GRADIENT):
        table[name] = vmem(3, NZ, *PLANE)
    table[TRANS_SUM] = vmem(NZ, *PLANE)
    table[EDGE] = vmem(6, 4, *PLANE)
    table[MID] = vmem(4, *PLANE)
    for level in (0, 1):
        planes = NZ >> level
        if level:
            table[COEF, level] = vmem(7, planes, *PLANE)
        for name in (SCALE, B, X, R):
            table[name, level] = vmem(planes, *PLANE)
    table[FACE] = vmem(3, 3, NZ, *PLANE)
    table[FACE_LOW, 0] = vmem(3, *PLANE)
    table[FACE_LOW, 1] = vmem(3, NZ, NX)
    table[FACE_LOW, 2] = vmem(3, NZ, *PLANE)
    table[OWN_COEF] = vmem(16, NX)
    table[ALL_COEF] = vmem(3, 4, 2 * REACH_Y + 1, 16, NX)
    table[OWN_B] = vmem(2, NX)
    table[ALL_B] = vmem(3, 4, 2 * REACH_Y + 1, 2, NX)
    for level in (2, 3):
        planes = 16 >> (level - 1)
        table[WIDE_COEF, level] = vmem(7, planes, *WIDE)
        for name in (WIDE_SCALE, WIDE_B, WIDE_R):
            table[name, level] = vmem(planes, *WIDE)
        table[WIDE_X, level] = vmem(planes + 2, *WIDE)
    for name in range(len(ROUNDS)):
        for dim in range(3):
            for up in (0, 1):
                table[SEND, name, dim, up] = vmem(*message_shape(name, dim, up))
                table[RECV, name, dim, up] = vmem(*message_shape(name, dim, up))
    table[OUT_SEM] = pltpu.SemaphoreType.DMA((4,))
    table[LOAD_SEM] = pltpu.SemaphoreType.DMA((len(shapes),))
    for name, count in ((SEND_SEM, 6 * len(ROUNDS)), (RECV_SEM, 6 * len(ROUNDS))):
        table[name] = pltpu.SemaphoreType.DMA((count,))
    for name in (COEF_SEM, B_SEM):
        table[name] = pltpu.SemaphoreType.DMA((2, len(PEERS)))
    return table


def rolled(value, amount, axis):
    amount = amount % value.shape[axis]
    return pltpu.roll(value, amount, axis) if amount else value


def kernel(sizes, scratch_names, *refs):
    hbm = refs[:12]
    adjoint_out, gradient_out = refs[12:14]
    ref = dict(zip(scratch_names, refs[14:]))
    adjoint_ref, gradient_ref = ref[ADJOINT], ref[GRADIENT]

    me = [lax.axis_index(axis) for axis in AXES]
    above = [lax.rem(me[d] + 1, sizes[d]) for d in range(3)]
    below = [lax.rem(me[d] + sizes[d] - 1, sizes[d]) for d in range(3)]

    loads = {}
    for name in LOAD_ORDER:
        loads[name] = pltpu.make_async_copy(
            hbm[name], ref[LOADED, name], ref[LOAD_SEM].at[name]
        )
        loads[name].start()

    peer_x = {a: lax.rem(me[2] + (a + sizes[2]), sizes[2]) for a in (-1, 1)} | {0: me[2]}
    peer_y = {b: lax.rem(me[1] + (b + sizes[1]), sizes[1]) for b in range(-REACH_Y, REACH_Y + 1)}
    peer_z = {c: lax.rem(me[0] + c, sizes[0]) for c in range(1, 4)} | {0: me[0]}
    peer_y[0] = me[1]

    def peer_of(offset):
        a, b, c = offset
        return (peer_x[a], peer_y[b], peer_z[c])

    barrier = pltpu.get_barrier_semaphore()
    for d in range(3):
        for peer in (above[d], below[d]):
            pl.semaphore_signal(barrier, inc=1, device_id={AXES[d]: peer}, device_id_type=MESH)

    low_on = [jnp.where(me[d] > 0, 1.0, 0.0).astype(jnp.float32) for d in range(3)]
    high_on = [jnp.where(me[d] < sizes[d] - 1, 1.0, 0.0).astype(jnp.float32) for d in range(3)]

    row = lax.broadcasted_iota(jnp.int32, PLANE, 0)
    lane = lax.broadcasted_iota(jnp.int32, PLANE, 1)
    zero = jnp.zeros(PLANE, jnp.float32)
    copies = []
    arrivals = {}

    def send(name, dim):
        for up in (1, 0):
            k = name * 6 + dim * 2 + up
            copy = pltpu.make_async_remote_copy(
                src_ref=ref[SEND, name, dim, up],
                dst_ref=ref[RECV, name, dim, up],
                send_sem=ref[SEND_SEM].at[k],
                recv_sem=ref[RECV_SEM].at[k],
                device_id={AXES[dim]: above[dim] if up else below[dim]},
                device_id_type=MESH,
            )
            copy.start()
            copies.append(copy)
            arrivals[name, dim, up] = copy

    def receive(name):
        for dim in range(3):
            for up in (1, 0):
                arrivals[name, dim, up].wait_recv()

    def offset(field, z, stride):
        return field * NZ + z * stride

    def packed(current, value, up, field, z, stride):
        at = offset(field, z, stride)
        moved = rolled(value, at + stride if up else at, 1)
        return jnp.where((lane >= at) & (lane < at + stride), moved, current)

    def halo_y(name, up, field, z):
        on = low_on[1] if up else high_on[1]
        return ref[RECV, name, 1, up][field, z : z + 1, :] * on

    def halo_x(name, up, field, z, stride):
        at = offset(field, z, stride)
        pack = ref[RECV, name, 2, up][...] * (low_on[2] if up else high_on[2])
        return rolled(pack, NX - at if up else 2 * NX - stride - at, 1)

    def halo_z(name, up, field):
        return ref[RECV, name, 0, up][field] * (low_on[0] if up else high_on[0])

    def at_low(dim, value, stride):
        return jnp.where((row if dim == 1 else lane) < stride, value, 0.0)

    def at_high(dim, value, stride):
        return jnp.where((row if dim == 1 else lane) >= PLANE[dim - 1] - stride, value, 0.0)

    def from_low(dim, value, stride):
        return jnp.where(
            (row if dim == 1 else lane) < stride, 0.0, rolled(value, stride, dim - 1)
        )

    def from_high(dim, value, stride):
        size = PLANE[dim - 1]
        return jnp.where(
            (row if dim == 1 else lane) >= size - stride, 0.0, rolled(value, -stride, dim - 1)
        )

    trans, blocks, inverses = ref[LOADED, TRANS], ref[LOADED, BLOCKS], ref[LOADED, INVERSES]
    iterate, rhs, total = ref[ITERATE], ref[RHS], ref[TOTAL]

    def smoothed(residual, z):
        return [
            inverses[c, z] * residual[0]
            + inverses[3 + c, z] * residual[1]
            + inverses[6 + c, z] * residual[2]
            for c in range(3)
        ]

    def send_iterate(name, channels):
        first = name == FIRST
        for c in range(channels):
            ref[SEND, name, 0, 1][c] = trans[0, NZ - 1] * iterate[c, NZ - 1]
            ref[SEND, name, 0, 0][c] = iterate[c, 0]
        if first:
            ref[SEND, name, 0, 1][channels] = trans[0, NZ - 1]
        send(name, 0)
        for z in range(NZ):
            coef = trans[1, z, NY - 1 : NY, :]
            for c in range(channels):
                ref[SEND, name, 1, 1][c, z : z + 1, :] = coef * iterate[c, z, NY - 1 : NY, :]
                ref[SEND, name, 1, 0][c, z : z + 1, :] = iterate[c, z, 0:1, :]
            if first:
                ref[SEND, name, 1, 1][channels, z : z + 1, :] = coef
        send(name, 1)
        high, low = zero, zero
        for z in range(NZ):
            coef = trans[2, z]
            for c in range(channels):
                high = packed(high, coef * iterate[c, z], 1, c, z, 1)
                low = packed(low, iterate[c, z], 0, c, z, 1)
            if first:
                high = packed(high, coef, 1, channels, z, 1)
        ref[SEND, name, 2, 1][...] = high
        ref[SEND, name, 2, 0][...] = low
        send(name, 2)

    def system_inside(channels):
        for z in range(NZ):
            values = [iterate[c, z] for c in range(3)]
            for c in range(channels):
                value = values[c]
                acc = (
                    blocks[c, z] * values[0]
                    + blocks[3 + c, z] * values[1]
                    + blocks[6 + c, z] * values[2]
                )
                if z > 0:
                    acc = acc - trans[0, z - 1] * iterate[c, z - 1]
                if z < NZ - 1:
                    acc = acc - trans[0, z] * iterate[c, z + 1]
                for dim in (1, 2):
                    coef = trans[dim, z]
                    acc = acc - from_low(dim, coef * value, 1)
                    acc = acc - coef * from_high(dim, value, 1)
                total[c, z] = acc

    def system_row(name, c, z):
        acc = total[c, z] + ref[TRANS_SUM][z] * iterate[c, z]
        if z == 0:
            acc = acc - halo_z(name, 1, c)
        if z == NZ - 1:
            acc = acc - trans[0, z] * halo_z(name, 0, c)
        acc = acc - at_low(1, halo_y(name, 1, c, z), 1)
        acc = acc - at_high(1, trans[1, z] * halo_y(name, 0, c, z), 1)
        acc = acc - at_low(2, halo_x(name, 1, c, z, 1), 1)
        acc = acc - at_high(2, trans[2, z] * halo_x(name, 0, c, z, 1), 1)
        return acc

    def trans_sum_inside():
        for z in range(NZ):
            acc = trans[0, z] + trans[1, z] + trans[2, z]
            if z > 0:
                acc = acc + trans[0, z - 1]
            for dim in (1, 2):
                acc = acc + from_low(dim, trans[dim, z], 1)
            ref[TRANS_SUM][z] = acc

    def trans_sum_rims():
        for z in range(NZ):
            acc = ref[TRANS_SUM][z]
            if z == 0:
                acc = acc + halo_z(FIRST, 1, 3)
            acc = acc + at_low(1, halo_y(FIRST, 1, 3, z), 1)
            acc = acc + at_low(2, halo_x(FIRST, 1, 3, z, 1), 1)
            ref[TRANS_SUM][z] = acc

    def coef(level, k, z):
        return ref[LOADED, FINE][k, z] if level == 0 else ref[COEF, level][k, z]

    def spread_level(level):
        rows, lanes = NY >> level, NX >> level
        source = ref[LOADED, ONE]
        pick = lax.broadcasted_iota(jnp.int32, (8, NX), 1) // (1 << level)
        for z in range(NZ >> level):
            for k in range(7):
                value = source[k, z]
                value = jnp.concatenate([value] * (1 << level), axis=1)
                if rows < 8:
                    value = jnp.concatenate([value] * (8 // rows), axis=0)
                value = jnp.take_along_axis(value, pick, axis=1, mode="promise_in_bounds")
                wide = jnp.broadcast_to(value[0:1], PLANE)
                for y in range(1, rows):
                    wide = jnp.where(row < y << level, wide, jnp.broadcast_to(value[y : y + 1], PLANE))
                ref[COEF, level][k, z] = wide

    def scales(level):
        for z in range(NZ >> level):
            ref[SCALE, level][z] = OMEGA / coef(level, 0, z)

    def send_level(name, level):
        planes, stride = NZ >> level, 1 << level
        x = [1.0] * planes if name in (RIMS, RIMS0) else ref[X, level]
        ref[SEND, name, 0, 1][0] = coef(level, 2, planes - 1) * x[planes - 1]
        ref[SEND, name, 0, 0][0] = coef(level, 1, 0) * x[0]
        send(name, 0)
        for z in range(planes):
            ref[SEND, name, 1, 1][0, z : z + 1, :] = (coef(level, 4, z) * x[z])[NY - 1 : NY]
            ref[SEND, name, 1, 0][0, z : z + 1, :] = (coef(level, 3, z) * x[z])[0:1]
        send(name, 1)
        high, low = zero, zero
        for z in range(planes):
            high = packed(high, coef(level, 6, z) * x[z], 1, 0, z, stride)
            low = packed(low, coef(level, 5, z) * x[z], 0, 0, z, stride)
        ref[SEND, name, 2, 1][...] = high
        ref[SEND, name, 2, 0][...] = low
        send(name, 2)

    def residual_inside(level):
        planes, stride = NZ >> level, 1 << level
        x, b, r = ref[X, level], ref[B, level], ref[R, level]
        for z in range(planes):
            acc = b[z] - coef(level, 0, z) * x[z]
            if z > 0:
                acc = acc - coef(level, 2, z - 1) * x[z - 1]
            if z < planes - 1:
                acc = acc - coef(level, 1, z + 1) * x[z + 1]
            for dim in (1, 2):
                acc = acc - from_low(dim, coef(level, 2 * dim + 2, z) * x[z], stride)
                acc = acc - from_high(dim, coef(level, 2 * dim + 1, z) * x[z], stride)
            r[z] = acc

    def residual(name, level, z):
        planes, stride = NZ >> level, 1 << level
        acc = ref[R, level][z]
        if z == 0:
            acc = acc - halo_z(name, 1, 0)
        if z == planes - 1:
            acc = acc - halo_z(name, 0, 0)
        acc = acc - at_low(1, halo_y(name, 1, 0, z), stride)
        acc = acc - at_high(1, halo_y(name, 0, 0, z), stride)
        acc = acc - at_low(2, halo_x(name, 1, 0, z, stride), stride)
        acc = acc - at_high(2, halo_x(name, 0, 0, z, stride), stride)
        return acc

    def paired(value, stride):
        for dim, place in ((0, row), (1, lane)):
            upper = (place & stride) != 0
            value = value + jnp.where(
                upper, rolled(value, stride, dim), rolled(value, -stride, dim)
            )
        return value

    def send_fields(name, fields, planes, stride):
        for dim in range(3):
            for up in (1, 0):
                pack = zero
                for f, field in enumerate(fields(dim, up)):
                    if dim == 0:
                        ref[SEND, name, 0, up][f] = field[planes - 1 if up else 0]
                        continue
                    for z in range(planes):
                        if dim == 1:
                            edge = field[z, NY - 1 : NY, :] if up else field[z, 0:1, :]
                            ref[SEND, name, 1, up][f, z : z + 1, :] = edge
                        else:
                            pack = packed(pack, field[z], up, f, z, stride)
                if dim == 2:
                    ref[SEND, name, 2, up][...] = pack
            send(name, dim)

    def edge_coefs():
        for z in range(4):
            scale = ref[SCALE, 1][z]
            low = [coef(1, 2, z - 1) if z > 0 else halo_z(RIMS, 1, 0)]
            high = [coef(1, 1, z + 1) if z < 3 else halo_z(RIMS, 0, 0)]
            low.append(from_low(1, coef(1, 4, z), 2) + at_low(1, halo_y(RIMS, 1, 0, z), 2))
            high.append(from_high(1, coef(1, 3, z), 2) + at_high(1, halo_y(RIMS, 0, 0, z), 2))
            low.append(from_low(2, coef(1, 6, z), 2) + at_low(2, halo_x(RIMS, 1, 0, z, 2), 2))
            high.append(from_high(2, coef(1, 5, z), 2) + at_high(2, halo_x(RIMS, 0, 0, z, 2), 2))
            for dim in range(3):
                ref[EDGE][2 * dim, z] = scale * low[dim]
                ref[EDGE][2 * dim + 1, z] = scale * high[dim]

    def edge_fields(dim, up):
        outer, inner = (2 * dim, 2 * dim + 1) if up else (2 * dim + 1, 2 * dim)
        order = [outer, inner] + [k for k in range(6) if k // 2 != dim]
        return [ref[EDGE].at[k] for k in order]

    row8 = lax.broadcasted_iota(jnp.int32, (8, NX), 0)
    lane8 = lax.broadcasted_iota(jnp.int32, (8, NX), 1)
    lane1 = lax.broadcasted_iota(jnp.int32, (1, NX), 1)
    windows = 2 * REACH_Y + 1

    def along_lanes(value, index):
        return jnp.take_along_axis(value, index, axis=1, mode="promise_in_bounds")

    def pack_own_coef():
        for k in range(7):
            place = lax.broadcasted_iota(jnp.int32, (4, NX), 0)
            lanes = lax.broadcasted_iota(jnp.int32, (4, NX), 1)
            for z in range(2):
                value = jnp.concatenate([ref[LOADED, TWO][k, z]] * 4, axis=1)
                value = jnp.where(lanes // 32 == place, value, 0.0)
                at = 2 * k + z
                ref[OWN_COEF][at : at + 1, :] = jnp.sum(value, axis=0, keepdims=True)
        place = lax.broadcasted_iota(jnp.int32, (2, NX), 0)
        lanes = lax.broadcasted_iota(jnp.int32, (2, NX), 1)
        for half in range(2):
            packed_row = jnp.zeros((1, NX), jnp.float32)
            for k in range(4 * half, min(7, 4 * half + 4)):
                value = jnp.concatenate([ref[LOADED, THREE][k, 0]] * 8, axis=1)
                value = jnp.where((lanes % 32) // 16 == place, value, 0.0)
                value = jnp.sum(value, axis=0, keepdims=True)
                packed_row = jnp.where(lane1 // 32 == k % 4, value, packed_row)
            ref[OWN_COEF][14 + half : 15 + half, :] = packed_row
        ref[ALL_COEF][1, me[0], REACH_Y] = ref[OWN_COEF][...]

    def pack_own_b(planes):
        for z, plane in enumerate(planes):
            total_row = jnp.zeros((8, NX), jnp.float32)
            for half in range(2):
                value = along_lanes(plane[8 * half : 8 * half + 8], 4 * (lane8 % 32))
                keep = (row8 % 4 == 0) & (row8 // 4 + 2 * half == lane8 // 32)
                total_row = total_row + jnp.where(keep, value, 0.0)
            ref[OWN_B][z : z + 1, :] = jnp.sum(total_row, axis=0, keepdims=True)
        ref[ALL_B][1, me[0], REACH_Y] = ref[OWN_B][...]

    def spread_to_peers(own, everyone, sems, chosen):
        for i in chosen:
            a, b, c = PEERS[i]
            copy = pltpu.make_async_remote_copy(
                src_ref=ref[own],
                dst_ref=ref[everyone].at[1 - a, me[0], REACH_Y - b],
                send_sem=ref[sems].at[0, i],
                recv_sem=ref[sems].at[1, i],
                device_id=peer_of(PEERS[i]),
                device_id_type=MESH,
            )
            copy.start()
            copies.append(copy)
            arrivals[sems, i] = copy

    def steps_away(steps):
        return [i for i, (a, b, c) in enumerate(PEERS) if abs(a) + abs(b) + min(c, 4 - c) == steps]

    def clear_unsent():
        for a in (-1, 0, 1):
            for b in range(-REACH_Y, REACH_Y + 1):
                for c in range(4):
                    if (a, b, c) not in PEERS + ((0, 0, 0),):
                        at = (a + 1, peer_z[c], b + REACH_Y)
                        ref[ALL_COEF][at] = jnp.zeros((16, NX), jnp.float32)
                        ref[ALL_B][at] = jnp.zeros((2, NX), jnp.float32)

    def receive_from_peers(sems):
        for i in range(len(PEERS)):
            arrivals[sems, i].wait_recv()

    def inside(value, size):
        return jnp.where((value >= 0) & (value < size), 1.0, 0.0).astype(jnp.float32)

    in_y = [inside(me[1] + (dy - REACH_Y), sizes[1]) for dy in range(windows)]
    in_x = [inside(me[2] + (dx - 1), sizes[2]) for dx in range(3)]

    def unpacked(everyone, layer, at, level, base, masked):
        width, rows = (32, row8 % 4) if level == 2 else (16, row8 % 4 // 2)
        step = 2 if level == 2 else 4
        start = base + rows * width
        middle = start + (lane8 - 32) // step
        sides = start + jnp.where(lane8 < 32, width // 2 + lane8 // step, (lane8 - 96) // step)
        tiles = []
        for t in range(4):
            halves = []
            for dy in (2 * t, 2 * t + 1):
                if dy >= windows:
                    blank = jnp.zeros((1, NX), jnp.float32)
                    halves.append((blank, blank))
                    continue
                left, own, right = [
                    ref[everyone][dx, layer, dy, at : at + 1, :] for dx in range(3)
                ]
                if masked:
                    left, own, right = (
                        left * (in_x[0] * in_y[dy]),
                        own * in_y[dy],
                        right * (in_x[2] * in_y[dy]),
                    )
                halves.append((own, jnp.where(lane1 % width < width // 2, right, left)))
            own, both = [
                jnp.where(
                    row8 < 4,
                    jnp.broadcast_to(halves[0][i], (8, NX)),
                    jnp.broadcast_to(halves[1][i], (8, NX)),
                )
                for i in range(2)
            ]
            tiles.append(
                jnp.where(
                    (lane8 >= 32) & (lane8 < 96),
                    along_lanes(own, jnp.clip(middle, 0, NX - 1)),
                    along_lanes(both, sides),
                )
            )
        return tiles

    def wide_coefs(level):
        for layer in range(4):
            for k in range(7):
                for zz in range(2 if level == 2 else 1):
                    at, base = (2 * k + zz, 0) if level == 2 else (14 + k // 4, k % 4 * 32)
                    plane = 2 * layer + zz if level == 2 else layer
                    for t, tile in enumerate(unpacked(ALL_COEF, layer, at, level, base, True)):
                        ref[WIDE_COEF, level][k, plane, 8 * t : 8 * t + 8, :] = tile
                        if k == 0:
                            live = tile > 0.0
                            ref[WIDE_SCALE, level][plane, 8 * t : 8 * t + 8, :] = jnp.where(
                                live, OMEGA / jnp.where(live, tile, 1.0), 0.0
                            )

    def wide_residual(level, z):
        planes = 16 >> (level - 1)
        rows, lanes = (1, 2) if level == 2 else (2, 4)
        a, x = ref[WIDE_COEF, level], ref[WIDE_X, level]
        acc = ref[WIDE_B, level][z] - a[0, z] * x[z + 1]
        if z > 0:
            acc = acc - a[2, z - 1] * x[z]
        if z < planes - 1:
            acc = acc - a[1, z + 1] * x[z + 2]
        for dim, stride in ((0, rows), (1, lanes)):
            acc = acc - rolled(a[2 * dim + 4, z] * x[z + 1], stride, dim)
            acc = acc - rolled(a[2 * dim + 3, z] * x[z + 1], -stride, dim)
        return acc

    def wide_relax(level):
        planes = 16 >> (level - 1)
        for z in range(planes):
            ref[WIDE_R, level][z] = wide_residual(level, z)
        x = ref[WIDE_X, level]
        for z in range(planes):
            x[z + 1] = x[z + 1] + ref[WIDE_SCALE, level][z] * ref[WIDE_R, level][z]

    def wide_start(level, z, value):
        ref[WIDE_B, level][z] = value
        ref[WIDE_X, level][z + 1] = ref[WIDE_SCALE, level][z] * value

    def wide_solve():
        wide_row = lax.broadcasted_iota(jnp.int32, WIDE, 0)
        wide_lane = lax.broadcasted_iota(jnp.int32, WIDE, 1)
        for layer in range(4):
            for zz in range(2):
                tiles = unpacked(ALL_B, layer, zz, 2, 0, False)
                wide_start(2, 2 * layer + zz, jnp.concatenate(tiles, axis=0))
        for z in range(4):
            pair = wide_residual(2, 2 * z) + wide_residual(2, 2 * z + 1)
            for dim, place, stride in ((0, wide_row, 1), (1, wide_lane, 2)):
                upper = (place & stride) != 0
                pair = pair + jnp.where(
                    upper, rolled(pair, stride, dim), rolled(pair, -stride, dim)
                )
            wide_start(3, z, pair)
        for sweep in range(COARSE_SWEEPS - 1):
            wide_relax(3)
        for z in range(8):
            ref[WIDE_X, 2][z + 1] = ref[WIDE_X, 2][z + 1] + ref[WIDE_X, 3][z // 2 + 1]

    def wide_final(plane):
        z = jnp.clip(plane, 0, 7)
        under, over = jnp.clip(plane - 1, 0, 7), jnp.clip(plane + 1, 0, 7)
        a, x = ref[WIDE_COEF, 2], ref[WIDE_X, 2]
        mid = slice(8, 24)
        acc = ref[WIDE_B, 2][z, mid] - a[0, z, mid] * x[z + 1, mid]
        acc = acc - a[2, under, mid] * x[z, mid]
        acc = acc - a[1, over, mid] * x[z + 2, mid]
        acc = acc - rolled(a[4, z] * x[z + 1], 1, 0)[mid]
        acc = acc - rolled(a[3, z] * x[z + 1], -1, 0)[mid]
        acc = acc - rolled(a[6, z, mid] * x[z + 1, mid], 2, 1)
        acc = acc - rolled(a[5, z, mid] * x[z + 1, mid], -2, 1)
        return (x[z + 1, mid] + ref[WIDE_SCALE, 2][z, mid] * acc) * inside(plane, 8)

    def onto_fine(wide_plane):
        value = wide_final(wide_plane - 1)
        tile, after = value[0:8], value[8:16]
        here = 32 + lane8 // 4 * 2

        def rows_of(value):
            wide = jnp.broadcast_to(value[4:5], PLANE)
            for y in range(1, 4):
                wide = jnp.where(row < 4 * y, wide, jnp.broadcast_to(value[4 + y : 5 + y], PLANE))
            return wide

        own = along_lanes(tile, here)
        left, right = along_lanes(tile, 31 + 0 * lane8), along_lanes(tile, 96 + 0 * lane8)
        after_left, after_right = (
            along_lanes(after, 31 + 0 * lane8),
            along_lanes(after, 96 + 0 * lane8),
        )
        return {
            "own": rows_of(own),
            "y": (along_lanes(after, here)[0:1], own[3:4]),
            "x": (rows_of(right), rows_of(left)),
            "corner": ((after_right[0:1], after_left[0:1]), (right[3:4], left[3:4])),
        }

    def level_one():
        c = [onto_fine(2 * me[0] + w) for w in range(4)]
        beside = []
        for w in range(4):
            own, (high_y, low_y), (high_x, low_x) = c[w]["own"], c[w]["y"], c[w]["x"]
            beside.append(
                (
                    from_low(1, own, 2) + at_low(1, low_y, 2),
                    from_high(1, own, 2) + at_high(1, high_y, 2),
                    from_low(2, own, 2) + at_low(2, low_x, 2),
                    from_high(2, own, 2) + at_high(2, high_x, 2),
                )
            )
        edge = ref[EDGE]
        for z in range(4):
            w = 1 + z // 2
            acc = ref[MID][z] + (1.0 - OMEGA) * c[w]["own"]
            acc = acc - edge[0, z] * c[1 + (z - 1) // 2]["own"]
            acc = acc - edge[1, z] * c[1 + (z + 1) // 2]["own"]
            for k in range(4):
                acc = acc - edge[2 + k, z] * beside[w][k]
            ref[X, 1][z] = acc
        rims = {}
        for up in (1, 0):
            w = 0 if up else 3
            f, here = ref[RECV, EDGES, 0, up], c[w]["own"]
            acc = ref[RECV, MIDDLE, 0, up][0] + (1.0 - OMEGA) * here - f[0] * here
            acc = acc - f[1] * c[1 if up else 2]["own"]
            for k in range(4):
                acc = acc - f[2 + k] * beside[w][k]
            rims[0, up] = acc
            side_y, side_x = [], []
            for z in range(4):
                w, w_low, w_high = 1 + z // 2, 1 + (z - 1) // 2, 1 + (z + 1) // 2
                f, here = ref[RECV, EDGES, 1, up], c[w]["y"][up]
                f = [f[k, z : z + 1, :] for k in range(6)]
                spread = jnp.broadcast_to(here, (8, NX))
                corner = c[w]["corner"][up]
                acc = ref[RECV, MIDDLE, 1, up][0, z : z + 1, :] + (1.0 - OMEGA) * here - f[0] * here
                acc = acc - f[1] * (c[w]["own"][0:1] if up else c[w]["own"][NY - 1 : NY])
                acc = acc - f[2] * c[w_low]["y"][up] - f[3] * c[w_high]["y"][up]
                acc = acc - f[4] * jnp.where(lane1 < 2, corner[1], rolled(spread, 2, 1)[0:1])
                acc = acc - f[5] * jnp.where(lane1 >= NX - 2, corner[0], rolled(spread, -2, 1)[0:1])
                side_y.append(acc)
                f = [halo_x(EDGES, up, k, z, 2) for k in range(6)]
                here = c[w]["x"][up]
                acc = halo_x(MIDDLE, up, 0, z, 2) + (1.0 - OMEGA) * here - f[0] * here
                acc = acc - f[1] * c[w]["own"]
                acc = acc - f[2] * c[w_low]["x"][up] - f[3] * c[w_high]["x"][up]
                acc = acc - f[4] * jnp.where(row < 2, c[w]["corner"][1][up], rolled(here, 2, 0))
                acc = acc - f[5] * jnp.where(row >= NY - 2, c[w]["corner"][0][up], rolled(here, -2, 0))
                side_x.append(acc)
            rims[1, up], rims[2, up] = side_y, side_x
        return rims

    saved, pressure = ref[LOADED, MOBILITIES], ref[LOADED, PRESSURE]

    def send_saved():
        name = SAVED
        fields = [lambda z, c=c: saved[c, z] for c in range(3)] + [lambda z: pressure[z]]
        for f, field in enumerate(fields):
            ref[SEND, name, 0, 1][f] = field(NZ - 1)
            ref[SEND, name, 0, 0][f] = field(0)
        send(name, 0)
        for f, field in enumerate(fields):
            for z in range(NZ):
                ref[SEND, name, 1, 1][f, z : z + 1, :] = field(z)[NY - 1 : NY]
                ref[SEND, name, 1, 0][f, z : z + 1, :] = field(z)[0:1]
        send(name, 1)
        high, low = zero, zero
        for f, field in enumerate(fields):
            for z in range(NZ):
                high = packed(high, field(z), 1, f, z, 1)
                low = packed(low, field(z), 0, f, z, 1)
        ref[SEND, name, 2, 1][...] = high
        ref[SEND, name, 2, 0][...] = low
        send(name, 2)

    def face_weights():
        name = SAVED
        receive(name)
        for z in range(NZ):
            p = pressure[z]
            for dim in range(3):
                if dim == 0:
                    high = pressure[z + 1] if z < NZ - 1 else halo_z(name, 0, 3)
                elif dim == 1:
                    high = from_high(1, p, 1) + at_high(1, halo_y(name, 0, 3, z), 1)
                else:
                    high = from_high(2, p, 1) + at_high(2, halo_x(name, 0, 3, z, 1), 1)
                step = 0.25 * trans[dim, z] * (p - high)
                for c in range(3):
                    m = saved[c, z]
                    if dim == 0:
                        high = saved[c, z + 1] if z < NZ - 1 else halo_z(name, 0, c)
                    elif dim == 1:
                        high = from_high(1, m, 1) + at_high(1, halo_y(name, 0, c, z), 1)
                    else:
                        high = from_high(2, m, 1) + at_high(2, halo_x(name, 0, c, z, 1), 1)
                    ref[FACE][dim, c, z] = step * (m + high)
            step = 0.25 * halo_y(FIRST, 1, 3, z) * (halo_y(name, 1, 3, z) - p[0:1])
            for c in range(3):
                ref[FACE_LOW, 1][c, z : z + 1, :] = step * (
                    halo_y(name, 1, c, z) + saved[c, z, 0:1, :]
                )
            step = 0.25 * halo_x(FIRST, 1, 3, z, 1) * (halo_x(name, 1, 3, z, 1) - p)
            for c in range(3):
                ref[FACE_LOW, 2][c, z] = step * (halo_x(name, 1, c, z, 1) + saved[c, z])
        step = 0.25 * halo_z(FIRST, 1, 3) * (halo_z(name, 1, 3) - pressure[0])
        for c in range(3):
            ref[FACE_LOW, 0][c] = step * (halo_z(name, 1, c) + saved[c, 0])

    loads[SOURCE].wait()
    loads[ACTIVE].wait()
    loads[INVERSES].wait()
    for z in range(NZ):
        mask = ref[LOADED, ACTIVE][z].astype(jnp.float32)
        values = [ref[LOADED, SOURCE][c, z] * mask for c in range(3)]
        for c in range(3):
            rhs[c, z] = values[c]
        for c, value in enumerate(smoothed(values, z)):
            iterate[c, z] = value
    loads[TRANS].wait()
    pl.semaphore_wait(barrier, 6)

    for name, channels in ((FIRST, 3), (SECOND, 3), (THIRD, 1)):
        send_iterate(name, channels)
        if name == FIRST:
            loads[BLOCKS].wait()
        system_inside(channels)
        if name == FIRST:
            trans_sum_inside()
            loads[TWO].wait()
            loads[THREE].wait()
            clear_unsent()
            pack_own_coef()
            spread_to_peers(OWN_COEF, ALL_COEF, COEF_SEM, steps_away(1))
            loads[ONE].wait()
            spread_level(1)
            scales(1)
        elif name == SECOND:
            spread_to_peers(OWN_COEF, ALL_COEF, COEF_SEM, steps_away(2))
            loads[FINE].wait()
            scales(0)
            send_level(RIMS, 1)
            send_level(RIMS0, 0)
        else:
            spread_to_peers(OWN_COEF, ALL_COEF, COEF_SEM, steps_away(3))
            loads[MOBILITIES].wait()
            loads[PRESSURE].wait()
            send_saved()
        receive(name)
        if name == FIRST:
            trans_sum_rims()
        for z in range(NZ):
            if name == THIRD:
                value = rhs[0, z] - system_row(name, 0, z)
                ref[B, 0][z] = value
                ref[X, 0][z] = ref[SCALE, 0][z] * value
            else:
                left = [rhs[c, z] - system_row(name, c, z) for c in range(3)]
                for c, value in enumerate(smoothed(left, z)):
                    iterate[c, z] = iterate[c, z] + value

    send_level(DOWN0, 0)
    residual_inside(0)
    spread_to_peers(OWN_COEF, ALL_COEF, COEF_SEM, steps_away(4))
    receive(RIMS)
    edge_coefs()
    send_fields(EDGES, edge_fields, 4, 2)
    receive(DOWN0)
    for z in range(4):
        pair = residual(DOWN0, 0, 2 * z) + residual(DOWN0, 0, 2 * z + 1)
        value = paired(pair, 1)
        ref[B, 1][z] = value
        ref[X, 1][z] = ref[SCALE, 1][z] * value

    send_level(DOWN1, 1)
    residual_inside(1)
    spread_to_peers(OWN_COEF, ALL_COEF, COEF_SEM, steps_away(5))
    face_weights()
    for level, planes in ((2, 8), (3, 4)):
        for z in (0, planes + 1):
            ref[WIDE_X, level][z] = jnp.zeros(WIDE, jnp.float32)
    receive(DOWN1)
    left = [residual(DOWN1, 1, z) for z in range(4)]
    pack_own_b([paired(left[2 * z] + left[2 * z + 1], 2) for z in range(2)])
    for z in range(4):
        ref[MID][z] = ref[X, 1][z] + ref[SCALE, 1][z] * left[z]

    spread_to_peers(OWN_B, ALL_B, B_SEM, [i for n in (5, 4, 3, 2, 1) for i in steps_away(n)])
    send_fields(MIDDLE, lambda dim, up: [ref[MID]], 4, 2)
    receive_from_peers(COEF_SEM)
    wide_coefs(2)
    wide_coefs(3)
    receive(RIMS0)
    receive(EDGES)
    receive(MIDDLE)
    receive_from_peers(B_SEM)
    wide_solve()

    rims = level_one()
    for z in range(NZ):
        ref[X, 0][z] = ref[X, 0][z] + ref[X, 1][z // 2]
    residual_inside(0)
    for z in range(NZ):
        acc = residual(DOWN0, 0, z)
        if z == 0:
            acc = acc - halo_z(RIMS0, 1, 0) * rims[0, 1]
        if z == NZ - 1:
            acc = acc - halo_z(RIMS0, 0, 0) * rims[0, 0]
        acc = acc - at_low(1, halo_y(RIMS0, 1, 0, z) * rims[1, 1][z // 2], 1)
        acc = acc - at_high(1, halo_y(RIMS0, 0, 0, z) * rims[1, 0][z // 2], 1)
        acc = acc - at_low(2, halo_x(RIMS0, 1, 0, z, 1) * rims[2, 1][z // 2], 1)
        acc = acc - at_high(2, halo_x(RIMS0, 0, 0, z, 1) * rims[2, 0][z // 2], 1)
        ref[R, 0][z] = acc
    for z in range(NZ):
        ref[X, 0][z] = ref[X, 0][z] + ref[SCALE, 0][z] * ref[R, 0][z]

    loads[WEIGHTS].wait()
    name = LAST
    stores = [pltpu.make_async_copy(adjoint_ref, adjoint_out, ref[OUT_SEM].at[3])]
    for dim in range(3):
        stores.append(
            pltpu.make_async_copy(gradient_ref.at[dim], gradient_out.at[dim], ref[OUT_SEM].at[dim])
        )
    for z in range(NZ):
        mask = ref[LOADED, ACTIVE][z].astype(jnp.float32)
        for c in range(3):
            adjoint_ref[c, z] = mask * (iterate[c, z] + ref[LOADED, WEIGHTS][c, z] * ref[X, 0][z])
    for c in range(3):
        ref[SEND, name, 0, 1][c] = adjoint_ref[c, NZ - 1]
        ref[SEND, name, 0, 0][c] = adjoint_ref[c, 0]
    send(name, 0)
    for z in range(NZ):
        for c in range(3):
            ref[SEND, name, 1, 1][c, z : z + 1, :] = adjoint_ref[c, z, NY - 1 : NY, :]
            ref[SEND, name, 1, 0][c, z : z + 1, :] = adjoint_ref[c, z, 0:1, :]
    send(name, 1)
    high, low = zero, zero
    for z in range(NZ):
        for c in range(3):
            high = packed(high, adjoint_ref[c, z], 1, c, z, 1)
            low = packed(low, adjoint_ref[c, z], 0, c, z, 1)
    ref[SEND, name, 2, 1][...] = high
    ref[SEND, name, 2, 0][...] = low
    send(name, 2)

    stores[0].start()
    face = ref[FACE]
    for dim in range(3):
        previous = None
        for z in range(NZ):
            flux = None
            for c in range(3):
                value = adjoint_ref[c, z]
                if dim == 0:
                    drop = value - adjoint_ref[c, z + 1] if z < NZ - 1 else value
                else:
                    drop = value - from_high(dim, value, 1)
                term = face[dim, c, z] * drop
                flux = term if flux is None else flux + term
            if dim == 0:
                gradient_ref[dim, z] = flux if previous is None else flux + previous
                previous = flux
            else:
                gradient_ref[dim, z] = flux + from_low(dim, flux, 1)
    for copy in copies[:-6]:
        copy.wait_send()
    receive(name)
    low_z, high_z = zero, zero
    for c in range(3):
        low_z = low_z + ref[FACE_LOW, 0][c] * (halo_z(name, 1, c) - adjoint_ref[c, 0])
        high_z = high_z + face[0, c, NZ - 1] * halo_z(name, 0, c)
    gradient_ref[0, 0] = gradient_ref[0, 0] + low_z
    gradient_ref[0, NZ - 1] = gradient_ref[0, NZ - 1] - high_z
    stores[1].start()
    for dim, halo in ((1, lambda *at: halo_y(name, *at)), (2, lambda *at: halo_x(name, *at, 1))):
        for z in range(NZ):
            low, high = zero, zero
            for c in range(3):
                rim = ref[FACE_LOW, 1][c, z : z + 1, :] if dim == 1 else ref[FACE_LOW, 2][c, z]
                low = low + rim * (halo(1, c, z) - adjoint_ref[c, z])
                high = high + face[dim, c, z] * halo(0, c, z)
            gradient_ref[dim, z] = gradient_ref[dim, z] + at_low(dim, low, 1) - at_high(dim, high, 1)
        stores[1 + dim].start()
    for store in stores:
        store.wait()
    for copy in copies[-6:]:
        copy.wait_send()


def hand_over(adjoint_in, gradient_in, adjoint_out, gradient_out, buffer, sems):
    arrays = ((adjoint_in, adjoint_out), (gradient_in, gradient_out))
    chunks = [(i, c) for i in range(2) for c in range(3)]
    loads = [
        pltpu.make_async_copy(arrays[i][0].at[c], buffer.at[i, c], sems.at[0, 3 * i + c])
        for i, c in chunks
    ]
    stores = [
        pltpu.make_async_copy(buffer.at[i, c], arrays[i][1].at[c], sems.at[1, 3 * i + c])
        for i, c in chunks
    ]
    for load in loads:
        load.start()
    for load, store in zip(loads, stores):
        load.wait()
        store.start()
    for store in stores:
        store.wait()


def solution(mesh):
    sizes = [mesh.shape[axis] for axis in AXES]

    def local(*args):
        table = scratch_table([(arg.shape, arg.dtype) for arg in args])
        out = jax.ShapeDtypeStruct((3, NZ) + PLANE, jnp.float32)
        results = pl.pallas_call(
            functools.partial(kernel, sizes, tuple(table)),
            out_shape=(out, out),
            in_specs=[pl.BlockSpec(memory_space=pl.ANY)] * len(args),
            out_specs=(pl.BlockSpec(memory_space=pl.ANY),) * 2,
            scratch_shapes=list(table.values()),
            compiler_params=pltpu.CompilerParams(collective_id=0, has_side_effects=True),
        )(*args)
        return pl.pallas_call(
            hand_over,
            out_shape=(out, out),
            in_specs=[pl.BlockSpec(memory_space=pl.ANY)] * 2,
            out_specs=(pl.BlockSpec(memory_space=pl.ANY),) * 2,
            scratch_shapes=[
                pltpu.VMEM((2, 3, NZ) + PLANE, jnp.float32),
                pltpu.SemaphoreType.DMA((2, 6)),
            ],
        )(*results)

    field = P("layer", "gy", "gx")
    stacked = P(None, "layer", "gy", "gx")
    return jax.shard_map(
        local,
        mesh=mesh,
        in_specs=(stacked, field) + (stacked,) * 8 + (field, stacked),
        out_specs=(stacked, stacked),
        check_vma=False,
    )
```

```python
import functools

import jax
import jax.numpy as jnp
from jax import lax
from jax.experimental import pallas as pl
from jax.experimental.pallas import tpu as pltpu
from jax.sharding import PartitionSpec as P

MESH = pl.DeviceIdType.MESH
OMEGA = 0.8
COARSE_SWEEPS = 4
AXES = ("layer", "gy", "gx")
NZ, NY, NX = 8, 16, 128
PLANE = (NY, NX)

FIRST, SECOND, THIRD, SAVED, RIMS, RIMS0, EDGES, DOWN0, DOWN1, MIDDLE, LAST = range(11)
ROUNDS = (
    (4, 3, 8),
    (3, 3, 8),
    (1, 1, 8),
    (4, 4, 8),
    (1, 1, 4),
    (1, 1, 8),
    (6, 6, 4),
    (1, 1, 8),
    (1, 1, 4),
    (1, 1, 4),
    (3, 3, 8),
)

(SOURCE, ACTIVE, BLOCKS, INVERSES, TRANS, WEIGHTS, FINE, ONE, TWO, THREE, PRESSURE, MOBILITIES) = range(12)
LOAD_ORDER = (SOURCE, ACTIVE, INVERSES, TRANS, BLOCKS, TWO, THREE, ONE, FINE, MOBILITIES, PRESSURE, WEIGHTS)

(
    LOADED,
    SEND,
    RECV,
    RHS,
    ITERATE,
    TOTAL,
    TRANS_SUM,
    COEF,
    SCALE,
    B,
    X,
    R,
    FACE,
    FACE_LOW,
    OWN_COEF,
    ALL_COEF,
    OWN_B,
    ALL_B,
    WIDE_COEF,
    WIDE_SCALE,
    WIDE_B,
    WIDE_X,
    WIDE_R,
    LOAD_SEM,
    SEND_SEM,
    RECV_SEM,
    COEF_SEM,
    B_SEM,
    ADJOINT,
    GRADIENT,
    OUT_SEM,
    EDGE,
    MID,
) = range(33)

WIDE = (32, 128)
REACH_Y = 3
PEERS = tuple(
    (a, b, c)
    for b in range(-REACH_Y, REACH_Y + 1)
    for a in (-1, 0, 1)
    for c in range(4)
    if (a, b, c) != (0, 0, 0)
    and (abs(b) < 3 or c != 2)
)


def message_shape(name, dim, up):
    fields_up, fields_down, planes = ROUNDS[name]
    fields = fields_up if up else fields_down
    if dim == 0:
        return (fields, NY, NX)
    if dim == 1:
        return (fields, planes, NX)
    return PLANE


def scratch_table(shapes):
    def vmem(*shape):
        return pltpu.VMEM(shape, jnp.float32)

    table = {}
    for name, (shape, dtype) in enumerate(shapes):
        table[LOADED, name] = pltpu.VMEM(shape, dtype)
    for name in (RHS, ITERATE, TOTAL, ADJOINT, GRADIENT):
        table[name] = vmem(3, NZ, *PLANE)
    table[TRANS_SUM] = vmem(NZ, *PLANE)
    table[EDGE] = vmem(6, 4, *PLANE)
    table[MID] = vmem(4, *PLANE)
    for level in (0, 1):
        planes = NZ >> level
        if level:
            table[COEF, level] = vmem(7, planes, *PLANE)
        for name in (SCALE, B, X, R):
            table[name, level] = vmem(planes, *PLANE)
    table[FACE] = vmem(3, 3, NZ, *PLANE)
    table[FACE_LOW, 0] = vmem(3, *PLANE)
    table[FACE_LOW, 1] = vmem(3, NZ, NX)
    table[FACE_LOW, 2] = vmem(3, NZ, *PLANE)
    table[OWN_COEF] = vmem(16, NX)
    table[ALL_COEF] = vmem(3, 4, 2 * REACH_Y + 1, 16, NX)
    table[OWN_B] = vmem(2, NX)
    table[ALL_B] = vmem(3, 4, 2 * REACH_Y + 1, 2, NX)
    for level in (2, 3):
        planes = 16 >> (level - 1)
        table[WIDE_COEF, level] = vmem(7, planes, *WIDE)
        for name in (WIDE_SCALE, WIDE_B, WIDE_R):
            table[name, level] = vmem(planes, *WIDE)
        table[WIDE_X, level] = vmem(planes + 2, *WIDE)
    for name in range(len(ROUNDS)):
        for dim in range(3):
            for up in (0, 1):
                table[SEND, name, dim, up] = vmem(*message_shape(name, dim, up))
                table[RECV, name, dim, up] = vmem(*message_shape(name, dim, up))
    table[OUT_SEM] = pltpu.SemaphoreType.DMA((4,))
    table[LOAD_SEM] = pltpu.SemaphoreType.DMA((len(shapes),))
    for name, count in ((SEND_SEM, 6 * len(ROUNDS)), (RECV_SEM, 6 * len(ROUNDS))):
        table[name] = pltpu.SemaphoreType.DMA((count,))
    for name in (COEF_SEM, B_SEM):
        table[name] = pltpu.SemaphoreType.DMA((2, len(PEERS)))
    return table


def rolled(value, amount, axis):
    amount = amount % value.shape[axis]
    return pltpu.roll(value, amount, axis) if amount else value


def kernel(sizes, scratch_names, *refs):
    hbm = refs[:12]
    adjoint_out, gradient_out = refs[12:14]
    ref = dict(zip(scratch_names, refs[14:]))
    adjoint_ref, gradient_ref = ref[ADJOINT], ref[GRADIENT]

    me = [lax.axis_index(axis) for axis in AXES]
    above = [lax.rem(me[d] + 1, sizes[d]) for d in range(3)]
    below = [lax.rem(me[d] + sizes[d] - 1, sizes[d]) for d in range(3)]

    loads = {}
    for name in LOAD_ORDER:
        loads[name] = pltpu.make_async_copy(
            hbm[name], ref[LOADED, name], ref[LOAD_SEM].at[name]
        )
        loads[name].start()

    peer_x = {a: lax.rem(me[2] + (a + sizes[2]), sizes[2]) for a in (-1, 1)} | {0: me[2]}
    peer_y = {b: lax.rem(me[1] + (b + sizes[1]), sizes[1]) for b in range(-REACH_Y, REACH_Y + 1)}
    peer_z = {c: lax.rem(me[0] + c, sizes[0]) for c in range(1, 4)} | {0: me[0]}
    peer_y[0] = me[1]

    def peer_of(offset):
        a, b, c = offset
        return (peer_x[a], peer_y[b], peer_z[c])

    barrier = pltpu.get_barrier_semaphore()
    for d in range(3):
        for peer in (above[d], below[d]):
            pl.semaphore_signal(barrier, inc=1, device_id={AXES[d]: peer}, device_id_type=MESH)

    low_on = [jnp.where(me[d] > 0, 1.0, 0.0).astype(jnp.float32) for d in range(3)]
    high_on = [jnp.where(me[d] < sizes[d] - 1, 1.0, 0.0).astype(jnp.float32) for d in range(3)]

    row = lax.broadcasted_iota(jnp.int32, PLANE, 0)
    lane = lax.broadcasted_iota(jnp.int32, PLANE, 1)
    zero = jnp.zeros(PLANE, jnp.float32)
    copies = []
    arrivals = {}

    def send(name, dim):
        for up in (1, 0):
            k = name * 6 + dim * 2 + up
            copy = pltpu.make_async_remote_copy(
                src_ref=ref[SEND, name, dim, up],
                dst_ref=ref[RECV, name, dim, up],
                send_sem=ref[SEND_SEM].at[k],
                recv_sem=ref[RECV_SEM].at[k],
                device_id={AXES[dim]: above[dim] if up else below[dim]},
                device_id_type=MESH,
            )
            copy.start()
            copies.append(copy)
            arrivals[name, dim, up] = copy

    def receive(name):
        for dim in range(3):
            for up in (1, 0):
                arrivals[name, dim, up].wait_recv()

    def offset(field, z, stride):
        return field * NZ + z * stride

    def packed(current, value, up, field, z, stride):
        at = offset(field, z, stride)
        moved = rolled(value, at + stride if up else at, 1)
        return jnp.where((lane >= at) & (lane < at + stride), moved, current)

    def halo_y(name, up, field, z):
        on = low_on[1] if up else high_on[1]
        return ref[RECV, name, 1, up][field, z : z + 1, :] * on

    def halo_x(name, up, field, z, stride):
        at = offset(field, z, stride)
        pack = ref[RECV, name, 2, up][...] * (low_on[2] if up else high_on[2])
        return rolled(pack, NX - at if up else 2 * NX - stride - at, 1)

    def halo_z(name, up, field):
        return ref[RECV, name, 0, up][field] * (low_on[0] if up else high_on[0])

    def at_low(dim, value, stride):
        return jnp.where((row if dim == 1 else lane) < stride, value, 0.0)

    def at_high(dim, value, stride):
        return jnp.where((row if dim == 1 else lane) >= PLANE[dim - 1] - stride, value, 0.0)

    def from_low(dim, value, stride):
        return jnp.where(
            (row if dim == 1 else lane) < stride, 0.0, rolled(value, stride, dim - 1)
        )

    def from_high(dim, value, stride):
        size = PLANE[dim - 1]
        return jnp.where(
            (row if dim == 1 else lane) >= size - stride, 0.0, rolled(value, -stride, dim - 1)
        )

    trans, blocks, inverses = ref[LOADED, TRANS], ref[LOADED, BLOCKS], ref[LOADED, INVERSES]
    iterate, rhs, total = ref[ITERATE], ref[RHS], ref[TOTAL]

    def smoothed(residual, z):
        return [
            inverses[c, z] * residual[0]
            + inverses[3 + c, z] * residual[1]
            + inverses[6 + c, z] * residual[2]
            for c in range(3)
        ]

    def send_iterate(name, channels):
        first = name == FIRST
        for c in range(channels):
            ref[SEND, name, 0, 1][c] = trans[0, NZ - 1] * iterate[c, NZ - 1]
            ref[SEND, name, 0, 0][c] = iterate[c, 0]
        if first:
            ref[SEND, name, 0, 1][channels] = trans[0, NZ - 1]
        send(name, 0)
        for z in range(NZ):
            coef = trans[1, z, NY - 1 : NY, :]
            for c in range(channels):
                ref[SEND, name, 1, 1][c, z : z + 1, :] = coef * iterate[c, z, NY - 1 : NY, :]
                ref[SEND, name, 1, 0][c, z : z + 1, :] = iterate[c, z, 0:1, :]
            if first:
                ref[SEND, name, 1, 1][channels, z : z + 1, :] = coef
        send(name, 1)
        high, low = zero, zero
        for z in range(NZ):
            coef = trans[2, z]
            for c in range(channels):
                high = packed(high, coef * iterate[c, z], 1, c, z, 1)
                low = packed(low, iterate[c, z], 0, c, z, 1)
            if first:
                high = packed(high, coef, 1, channels, z, 1)
        ref[SEND, name, 2, 1][...] = high
        ref[SEND, name, 2, 0][...] = low
        send(name, 2)

    def system_inside(channels):
        for z in range(NZ):
            values = [iterate[c, z] for c in range(3)]
            for c in range(channels):
                value = values[c]
                acc = (
                    blocks[c, z] * values[0]
                    + blocks[3 + c, z] * values[1]
                    + blocks[6 + c, z] * values[2]
                )
                if z > 0:
                    acc = acc - trans[0, z - 1] * iterate[c, z - 1]
                if z < NZ - 1:
                    acc = acc - trans[0, z] * iterate[c, z + 1]
                for dim in (1, 2):
                    coef = trans[dim, z]
                    acc = acc - from_low(dim, coef * value, 1)
                    acc = acc - coef * from_high(dim, value, 1)
                total[c, z] = acc

    def system_row(name, c, z):
        acc = total[c, z] + ref[TRANS_SUM][z] * iterate[c, z]
        if z == 0:
            acc = acc - halo_z(name, 1, c)
        if z == NZ - 1:
            acc = acc - trans[0, z] * halo_z(name, 0, c)
        acc = acc - at_low(1, halo_y(name, 1, c, z), 1)
        acc = acc - at_high(1, trans[1, z] * halo_y(name, 0, c, z), 1)
        acc = acc - at_low(2, halo_x(name, 1, c, z, 1), 1)
        acc = acc - at_high(2, trans[2, z] * halo_x(name, 0, c, z, 1), 1)
        return acc

    def trans_sum_inside():
        for z in range(NZ):
            acc = trans[0, z] + trans[1, z] + trans[2, z]
            if z > 0:
                acc = acc + trans[0, z - 1]
            for dim in (1, 2):
                acc = acc + from_low(dim, trans[dim, z], 1)
            ref[TRANS_SUM][z] = acc

    def trans_sum_rims():
        for z in range(NZ):
            acc = ref[TRANS_SUM][z]
            if z == 0:
                acc = acc + halo_z(FIRST, 1, 3)
            acc = acc + at_low(1, halo_y(FIRST, 1, 3, z), 1)
            acc = acc + at_low(2, halo_x(FIRST, 1, 3, z, 1), 1)
            ref[TRANS_SUM][z] = acc

    def coef(level, k, z):
        return ref[LOADED, FINE][k, z] if level == 0 else ref[COEF, level][k, z]

    def spread_level(level):
        rows, lanes = NY >> level, NX >> level
        source = ref[LOADED, ONE]
        pick = lax.broadcasted_iota(jnp.int32, (8, NX), 1) // (1 << level)
        for z in range(NZ >> level):
            for k in range(7):
                value = source[k, z]
                value = jnp.concatenate([value] * (1 << level), axis=1)
                if rows < 8:
                    value = jnp.concatenate([value] * (8 // rows), axis=0)
                value = jnp.take_along_axis(value, pick, axis=1, mode="promise_in_bounds")
                wide = jnp.broadcast_to(value[0:1], PLANE)
                for y in range(1, rows):
                    wide = jnp.where(row < y << level, wide, jnp.broadcast_to(value[y : y + 1], PLANE))
                ref[COEF, level][k, z] = wide

    def scales(level):
        for z in range(NZ >> level):
            ref[SCALE, level][z] = OMEGA / coef(level, 0, z)

    def send_level(name, level):
        planes, stride = NZ >> level, 1 << level
        x = [1.0] * planes if name in (RIMS, RIMS0) else ref[X, level]
        ref[SEND, name, 0, 1][0] = coef(level, 2, planes - 1) * x[planes - 1]
        ref[SEND, name, 0, 0][0] = coef(level, 1, 0) * x[0]
        send(name, 0)
        for z in range(planes):
            ref[SEND, name, 1, 1][0, z : z + 1, :] = (coef(level, 4, z) * x[z])[NY - 1 : NY]
            ref[SEND, name, 1, 0][0, z : z + 1, :] = (coef(level, 3, z) * x[z])[0:1]
        send(name, 1)
        high, low = zero, zero
        for z in range(planes):
            high = packed(high, coef(level, 6, z) * x[z], 1, 0, z, stride)
            low = packed(low, coef(level, 5, z) * x[z], 0, 0, z, stride)
        ref[SEND, name, 2, 1][...] = high
        ref[SEND, name, 2, 0][...] = low
        send(name, 2)

    def residual_inside(level):
        planes, stride = NZ >> level, 1 << level
        x, b, r = ref[X, level], ref[B, level], ref[R, level]
        for z in range(planes):
            acc = b[z] - coef(level, 0, z) * x[z]
            if z > 0:
                acc = acc - coef(level, 2, z - 1) * x[z - 1]
            if z < planes - 1:
                acc = acc - coef(level, 1, z + 1) * x[z + 1]
            for dim in (1, 2):
                acc = acc - from_low(dim, coef(level, 2 * dim + 2, z) * x[z], stride)
                acc = acc - from_high(dim, coef(level, 2 * dim + 1, z) * x[z], stride)
            r[z] = acc

    def residual(name, level, z):
        planes, stride = NZ >> level, 1 << level
        acc = ref[R, level][z]
        if z == 0:
            acc = acc - halo_z(name, 1, 0)
        if z == planes - 1:
            acc = acc - halo_z(name, 0, 0)
        acc = acc - at_low(1, halo_y(name, 1, 0, z), stride)
        acc = acc - at_high(1, halo_y(name, 0, 0, z), stride)
        acc = acc - at_low(2, halo_x(name, 1, 0, z, stride), stride)
        acc = acc - at_high(2, halo_x(name, 0, 0, z, stride), stride)
        return acc

    def paired(value, stride):
        for dim, place in ((0, row), (1, lane)):
            upper = (place & stride) != 0
            value = value + jnp.where(
                upper, rolled(value, stride, dim), rolled(value, -stride, dim)
            )
        return value

    def send_fields(name, fields, planes, stride):
        for dim in range(3):
            for up in (1, 0):
                pack = zero
                for f, field in enumerate(fields(dim, up)):
                    if dim == 0:
                        ref[SEND, name, 0, up][f] = field[planes - 1 if up else 0]
                        continue
                    for z in range(planes):
                        if dim == 1:
                            edge = field[z, NY - 1 : NY, :] if up else field[z, 0:1, :]
                            ref[SEND, name, 1, up][f, z : z + 1, :] = edge
                        else:
                            pack = packed(pack, field[z], up, f, z, stride)
                if dim == 2:
                    ref[SEND, name, 2, up][...] = pack
            send(name, dim)

    def edge_coefs():
        for z in range(4):
            scale = ref[SCALE, 1][z]
            low = [coef(1, 2, z - 1) if z > 0 else halo_z(RIMS, 1, 0)]
            high = [coef(1, 1, z + 1) if z < 3 else halo_z(RIMS, 0, 0)]
            low.append(from_low(1, coef(1, 4, z), 2) + at_low(1, halo_y(RIMS, 1, 0, z), 2))
            high.append(from_high(1, coef(1, 3, z), 2) + at_high(1, halo_y(RIMS, 0, 0, z), 2))
            low.append(from_low(2, coef(1, 6, z), 2) + at_low(2, halo_x(RIMS, 1, 0, z, 2), 2))
            high.append(from_high(2, coef(1, 5, z), 2) + at_high(2, halo_x(RIMS, 0, 0, z, 2), 2))
            for dim in range(3):
                ref[EDGE][2 * dim, z] = scale * low[dim]
                ref[EDGE][2 * dim + 1, z] = scale * high[dim]

    def edge_fields(dim, up):
        outer, inner = (2 * dim, 2 * dim + 1) if up else (2 * dim + 1, 2 * dim)
        order = [outer, inner] + [k for k in range(6) if k // 2 != dim]
        return [ref[EDGE].at[k] for k in order]

    row8 = lax.broadcasted_iota(jnp.int32, (8, NX), 0)
    lane8 = lax.broadcasted_iota(jnp.int32, (8, NX), 1)
    lane1 = lax.broadcasted_iota(jnp.int32, (1, NX), 1)
    windows = 2 * REACH_Y + 1

    def along_lanes(value, index):
        return jnp.take_along_axis(value, index, axis=1, mode="promise_in_bounds")

    def pack_own_coef():
        for k in range(7):
            place = lax.broadcasted_iota(jnp.int32, (4, NX), 0)
            lanes = lax.broadcasted_iota(jnp.int32, (4, NX), 1)
            for z in range(2):
                value = jnp.concatenate([ref[LOADED, TWO][k, z]] * 4, axis=1)
                value = jnp.where(lanes // 32 == place, value, 0.0)
                at = 2 * k + z
                ref[OWN_COEF][at : at + 1, :] = jnp.sum(value, axis=0, keepdims=True)
        place = lax.broadcasted_iota(jnp.int32, (2, NX), 0)
        lanes = lax.broadcasted_iota(jnp.int32, (2, NX), 1)
        for half in range(2):
            packed_row = jnp.zeros((1, NX), jnp.float32)
            for k in range(4 * half, min(7, 4 * half + 4)):
                value = jnp.concatenate([ref[LOADED, THREE][k, 0]] * 8, axis=1)
                value = jnp.where((lanes % 32) // 16 == place, value, 0.0)
                value = jnp.sum(value, axis=0, keepdims=True)
                packed_row = jnp.where(lane1 // 32 == k % 4, value, packed_row)
            ref[OWN_COEF][14 + half : 15 + half, :] = packed_row
        ref[ALL_COEF][1, me[0], REACH_Y] = ref[OWN_COEF][...]

    def pack_own_b(planes):
        for z, plane in enumerate(planes):
            total_row = jnp.zeros((8, NX), jnp.float32)
            for half in range(2):
                value = along_lanes(plane[8 * half : 8 * half + 8], 4 * (lane8 % 32))
                keep = (row8 % 4 == 0) & (row8 // 4 + 2 * half == lane8 // 32)
                total_row = total_row + jnp.where(keep, value, 0.0)
            ref[OWN_B][z : z + 1, :] = jnp.sum(total_row, axis=0, keepdims=True)
        ref[ALL_B][1, me[0], REACH_Y] = ref[OWN_B][...]

    def spread_to_peers(own, everyone, sems, chosen):
        for i in chosen:
            a, b, c = PEERS[i]
            copy = pltpu.make_async_remote_copy(
                src_ref=ref[own],
                dst_ref=ref[everyone].at[1 - a, me[0], REACH_Y - b],
                send_sem=ref[sems].at[0, i],
                recv_sem=ref[sems].at[1, i],
                device_id=peer_of(PEERS[i]),
                device_id_type=MESH,
            )
            copy.start()
            copies.append(copy)
            arrivals[sems, i] = copy

    def steps_away(steps):
        return [i for i, (a, b, c) in enumerate(PEERS) if abs(a) + abs(b) + min(c, 4 - c) == steps]

    def clear_unsent():
        for a in (-1, 0, 1):
            for b in range(-REACH_Y, REACH_Y + 1):
                for c in range(4):
                    if (a, b, c) not in PEERS + ((0, 0, 0),):
                        at = (a + 1, peer_z[c], b + REACH_Y)
                        ref[ALL_COEF][at] = jnp.zeros((16, NX), jnp.float32)
                        ref[ALL_B][at] = jnp.zeros((2, NX), jnp.float32)

    def receive_from_peers(sems):
        for i in range(len(PEERS)):
            arrivals[sems, i].wait_recv()

    def inside(value, size):
        return jnp.where((value >= 0) & (value < size), 1.0, 0.0).astype(jnp.float32)

    in_y = [inside(me[1] + (dy - REACH_Y), sizes[1]) for dy in range(windows)]
    in_x = [inside(me[2] + (dx - 1), sizes[2]) for dx in range(3)]

    def unpacked(everyone, layer, at, level, base, masked):
        width, rows = (32, row8 % 4) if level == 2 else (16, row8 % 4 // 2)
        step = 2 if level == 2 else 4
        start = base + rows * width
        middle = start + (lane8 - 32) // step
        sides = start + jnp.where(lane8 < 32, width // 2 + lane8 // step, (lane8 - 96) // step)
        tiles = []
        for t in range(4):
            halves = []
            for dy in (2 * t, 2 * t + 1):
                if dy >= windows:
                    blank = jnp.zeros((1, NX), jnp.float32)
                    halves.append((blank, blank))
                    continue
                left, own, right = [
                    ref[everyone][dx, layer, dy, at : at + 1, :] for dx in range(3)
                ]
                if masked:
                    left, own, right = (
                        left * (in_x[0] * in_y[dy]),
                        own * in_y[dy],
                        right * (in_x[2] * in_y[dy]),
                    )
                halves.append((own, jnp.where(lane1 % width < width // 2, right, left)))
            own, both = [
                jnp.where(
                    row8 < 4,
                    jnp.broadcast_to(halves[0][i], (8, NX)),
                    jnp.broadcast_to(halves[1][i], (8, NX)),
                )
                for i in range(2)
            ]
            tiles.append(
                jnp.where(
                    (lane8 >= 32) & (lane8 < 96),
                    along_lanes(own, jnp.clip(middle, 0, NX - 1)),
                    along_lanes(both, sides),
                )
            )
        return tiles

    def wide_coefs(level):
        for layer in range(4):
            for k in range(7):
                for zz in range(2 if level == 2 else 1):
                    at, base = (2 * k + zz, 0) if level == 2 else (14 + k // 4, k % 4 * 32)
                    plane = 2 * layer + zz if level == 2 else layer
                    for t, tile in enumerate(unpacked(ALL_COEF, layer, at, level, base, True)):
                        ref[WIDE_COEF, level][k, plane, 8 * t : 8 * t + 8, :] = tile
                        if k == 0:
                            live = tile > 0.0
                            ref[WIDE_SCALE, level][plane, 8 * t : 8 * t + 8, :] = jnp.where(
                                live, OMEGA / jnp.where(live, tile, 1.0), 0.0
                            )

    def wide_residual(level, z):
        planes = 16 >> (level - 1)
        rows, lanes = (1, 2) if level == 2 else (2, 4)
        a, x = ref[WIDE_COEF, level], ref[WIDE_X, level]
        acc = ref[WIDE_B, level][z] - a[0, z] * x[z + 1]
        if z > 0:
            acc = acc - a[2, z - 1] * x[z]
        if z < planes - 1:
            acc = acc - a[1, z + 1] * x[z + 2]
        for dim, stride in ((0, rows), (1, lanes)):
            acc = acc - rolled(a[2 * dim + 4, z] * x[z + 1], stride, dim)
            acc = acc - rolled(a[2 * dim + 3, z] * x[z + 1], -stride, dim)
        return acc

    def wide_relax(level):
        planes = 16 >> (level - 1)
        for z in range(planes):
            ref[WIDE_R, level][z] = wide_residual(level, z)
        x = ref[WIDE_X, level]
        for z in range(planes):
            x[z + 1] = x[z + 1] + ref[WIDE_SCALE, level][z] * ref[WIDE_R, level][z]

    def wide_start(level, z, value):
        ref[WIDE_B, level][z] = value
        ref[WIDE_X, level][z + 1] = ref[WIDE_SCALE, level][z] * value

    def wide_solve():
        wide_row = lax.broadcasted_iota(jnp.int32, WIDE, 0)
        wide_lane = lax.broadcasted_iota(jnp.int32, WIDE, 1)
        for layer in range(4):
            for zz in range(2):
                tiles = unpacked(ALL_B, layer, zz, 2, 0, False)
                wide_start(2, 2 * layer + zz, jnp.concatenate(tiles, axis=0))
        for z in range(4):
            pair = wide_residual(2, 2 * z) + wide_residual(2, 2 * z + 1)
            for dim, place, stride in ((0, wide_row, 1), (1, wide_lane, 2)):
                upper = (place & stride) != 0
                pair = pair + jnp.where(
                    upper, rolled(pair, stride, dim), rolled(pair, -stride, dim)
                )
            wide_start(3, z, pair)
        for sweep in range(COARSE_SWEEPS - 1):
            wide_relax(3)
        for z in range(8):
            ref[WIDE_X, 2][z + 1] = ref[WIDE_X, 2][z + 1] + ref[WIDE_X, 3][z // 2 + 1]

    def wide_final(plane):
        z = jnp.clip(plane, 0, 7)
        under, over = jnp.clip(plane - 1, 0, 7), jnp.clip(plane + 1, 0, 7)
        a, x = ref[WIDE_COEF, 2], ref[WIDE_X, 2]
        mid = slice(8, 24)
        acc = ref[WIDE_B, 2][z, mid] - a[0, z, mid] * x[z + 1, mid]
        acc = acc - a[2, under, mid] * x[z, mid]
        acc = acc - a[1, over, mid] * x[z + 2, mid]
        acc = acc - rolled(a[4, z] * x[z + 1], 1, 0)[mid]
        acc = acc - rolled(a[3, z] * x[z + 1], -1, 0)[mid]
        acc = acc - rolled(a[6, z, mid] * x[z + 1, mid], 2, 1)
        acc = acc - rolled(a[5, z, mid] * x[z + 1, mid], -2, 1)
        return (x[z + 1, mid] + ref[WIDE_SCALE, 2][z, mid] * acc) * inside(plane, 8)

    def onto_fine(wide_plane):
        value = wide_final(wide_plane - 1)
        tile, after = value[0:8], value[8:16]
        here = 32 + lane8 // 4 * 2

        def rows_of(value):
            wide = jnp.broadcast_to(value[4:5], PLANE)
            for y in range(1, 4):
                wide = jnp.where(row < 4 * y, wide, jnp.broadcast_to(value[4 + y : 5 + y], PLANE))
            return wide

        own = along_lanes(tile, here)
        left, right = along_lanes(tile, 31 + 0 * lane8), along_lanes(tile, 96 + 0 * lane8)
        after_left, after_right = (
            along_lanes(after, 31 + 0 * lane8),
            along_lanes(after, 96 + 0 * lane8),
        )
        return {
            "own": rows_of(own),
            "y": (along_lanes(after, here)[0:1], own[3:4]),
            "x": (rows_of(right), rows_of(left)),
            "corner": ((after_right[0:1], after_left[0:1]), (right[3:4], left[3:4])),
        }

    def level_one():
        c = [onto_fine(2 * me[0] + w) for w in range(4)]
        beside = []
        for w in range(4):
            own, (high_y, low_y), (high_x, low_x) = c[w]["own"], c[w]["y"], c[w]["x"]
            beside.append(
                (
                    from_low(1, own, 2) + at_low(1, low_y, 2),
                    from_high(1, own, 2) + at_high(1, high_y, 2),
                    from_low(2, own, 2) + at_low(2, low_x, 2),
                    from_high(2, own, 2) + at_high(2, high_x, 2),
                )
            )
        edge = ref[EDGE]
        for z in range(4):
            w = 1 + z // 2
            acc = ref[MID][z] + (1.0 - OMEGA) * c[w]["own"]
            acc = acc - edge[0, z] * c[1 + (z - 1) // 2]["own"]
            acc = acc - edge[1, z] * c[1 + (z + 1) // 2]["own"]
            for k in range(4):
                acc = acc - edge[2 + k, z] * beside[w][k]
            ref[X, 1][z] = acc
        rims = {}
        for up in (1, 0):
            w = 0 if up else 3
            f, here = ref[RECV, EDGES, 0, up], c[w]["own"]
            acc = ref[RECV, MIDDLE, 0, up][0] + (1.0 - OMEGA) * here - f[0] * here
            acc = acc - f[1] * c[1 if up else 2]["own"]
            for k in range(4):
                acc = acc - f[2 + k] * beside[w][k]
            rims[0, up] = acc
            side_y, side_x = [], []
            for z in range(4):
                w, w_low, w_high = 1 + z // 2, 1 + (z - 1) // 2, 1 + (z + 1) // 2
                f, here = ref[RECV, EDGES, 1, up], c[w]["y"][up]
                f = [f[k, z : z + 1, :] for k in range(6)]
                spread = jnp.broadcast_to(here, (8, NX))
                corner = c[w]["corner"][up]
                acc = ref[RECV, MIDDLE, 1, up][0, z : z + 1, :] + (1.0 - OMEGA) * here - f[0] * here
                acc = acc - f[1] * (c[w]["own"][0:1] if up else c[w]["own"][NY - 1 : NY])
                acc = acc - f[2] * c[w_low]["y"][up] - f[3] * c[w_high]["y"][up]
                acc = acc - f[4] * jnp.where(lane1 < 2, corner[1], rolled(spread, 2, 1)[0:1])
                acc = acc - f[5] * jnp.where(lane1 >= NX - 2, corner[0], rolled(spread, -2, 1)[0:1])
                side_y.append(acc)
                f = [halo_x(EDGES, up, k, z, 2) for k in range(6)]
                here = c[w]["x"][up]
                acc = halo_x(MIDDLE, up, 0, z, 2) + (1.0 - OMEGA) * here - f[0] * here
                acc = acc - f[1] * c[w]["own"]
                acc = acc - f[2] * c[w_low]["x"][up] - f[3] * c[w_high]["x"][up]
                acc = acc - f[4] * jnp.where(row < 2, c[w]["corner"][1][up], rolled(here, 2, 0))
                acc = acc - f[5] * jnp.where(row >= NY - 2, c[w]["corner"][0][up], rolled(here, -2, 0))
                side_x.append(acc)
            rims[1, up], rims[2, up] = side_y, side_x
        return rims

    saved, pressure = ref[LOADED, MOBILITIES], ref[LOADED, PRESSURE]

    def send_saved():
        name = SAVED
        fields = [lambda z, c=c: saved[c, z] for c in range(3)] + [lambda z: pressure[z]]
        for f, field in enumerate(fields):
            ref[SEND, name, 0, 1][f] = field(NZ - 1)
            ref[SEND, name, 0, 0][f] = field(0)
        send(name, 0)
        for f, field in enumerate(fields):
            for z in range(NZ):
                ref[SEND, name, 1, 1][f, z : z + 1, :] = field(z)[NY - 1 : NY]
                ref[SEND, name, 1, 0][f, z : z + 1, :] = field(z)[0:1]
        send(name, 1)
        high, low = zero, zero
        for f, field in enumerate(fields):
            for z in range(NZ):
                high = packed(high, field(z), 1, f, z, 1)
                low = packed(low, field(z), 0, f, z, 1)
        ref[SEND, name, 2, 1][...] = high
        ref[SEND, name, 2, 0][...] = low
        send(name, 2)

    def face_weights():
        name = SAVED
        receive(name)
        for z in range(NZ):
            p = pressure[z]
            for dim in range(3):
                if dim == 0:
                    high = pressure[z + 1] if z < NZ - 1 else halo_z(name, 0, 3)
                elif dim == 1:
                    high = from_high(1, p, 1) + at_high(1, halo_y(name, 0, 3, z), 1)
                else:
                    high = from_high(2, p, 1) + at_high(2, halo_x(name, 0, 3, z, 1), 1)
                step = 0.25 * trans[dim, z] * (p - high)
                for c in range(3):
                    m = saved[c, z]
                    if dim == 0:
                        high = saved[c, z + 1] if z < NZ - 1 else halo_z(name, 0, c)
                    elif dim == 1:
                        high = from_high(1, m, 1) + at_high(1, halo_y(name, 0, c, z), 1)
                    else:
                        high = from_high(2, m, 1) + at_high(2, halo_x(name, 0, c, z, 1), 1)
                    ref[FACE][dim, c, z] = step * (m + high)
            step = 0.25 * halo_y(FIRST, 1, 3, z) * (halo_y(name, 1, 3, z) - p[0:1])
            for c in range(3):
                ref[FACE_LOW, 1][c, z : z + 1, :] = step * (
                    halo_y(name, 1, c, z) + saved[c, z, 0:1, :]
                )
            step = 0.25 * halo_x(FIRST, 1, 3, z, 1) * (halo_x(name, 1, 3, z, 1) - p)
            for c in range(3):
                ref[FACE_LOW, 2][c, z] = step * (halo_x(name, 1, c, z, 1) + saved[c, z])
        step = 0.25 * halo_z(FIRST, 1, 3) * (halo_z(name, 1, 3) - pressure[0])
        for c in range(3):
            ref[FACE_LOW, 0][c] = step * (halo_z(name, 1, c) + saved[c, 0])

    loads[SOURCE].wait()
    loads[ACTIVE].wait()
    loads[INVERSES].wait()
    for z in range(NZ):
        mask = ref[LOADED, ACTIVE][z].astype(jnp.float32)
        values = [ref[LOADED, SOURCE][c, z] * mask for c in range(3)]
        for c in range(3):
            rhs[c, z] = values[c]
        for c, value in enumerate(smoothed(values, z)):
            iterate[c, z] = value
    loads[TRANS].wait()
    pl.semaphore_wait(barrier, 6)

    for name, channels in ((FIRST, 3), (SECOND, 3), (THIRD, 1)):
        send_iterate(name, channels)
        if name == FIRST:
            loads[BLOCKS].wait()
        system_inside(channels)
        if name == FIRST:
            trans_sum_inside()
            loads[TWO].wait()
            loads[THREE].wait()
            clear_unsent()
            pack_own_coef()
            spread_to_peers(OWN_COEF, ALL_COEF, COEF_SEM, steps_away(1))
            loads[ONE].wait()
            spread_level(1)
            scales(1)
        elif name == SECOND:
            spread_to_peers(OWN_COEF, ALL_COEF, COEF_SEM, steps_away(2))
            loads[FINE].wait()
            scales(0)
            send_level(RIMS, 1)
            send_level(RIMS0, 0)
        else:
            spread_to_peers(OWN_COEF, ALL_COEF, COEF_SEM, steps_away(3))
            loads[MOBILITIES].wait()
            loads[PRESSURE].wait()
            send_saved()
        receive(name)
        if name == FIRST:
            trans_sum_rims()
        for z in range(NZ):
            if name == THIRD:
                value = rhs[0, z] - system_row(name, 0, z)
                ref[B, 0][z] = value
                ref[X, 0][z] = ref[SCALE, 0][z] * value
            else:
                left = [rhs[c, z] - system_row(name, c, z) for c in range(3)]
                for c, value in enumerate(smoothed(left, z)):
                    iterate[c, z] = iterate[c, z] + value

    send_level(DOWN0, 0)
    residual_inside(0)
    spread_to_peers(OWN_COEF, ALL_COEF, COEF_SEM, steps_away(4))
    receive(RIMS)
    edge_coefs()
    send_fields(EDGES, edge_fields, 4, 2)
    receive(DOWN0)
    for z in range(4):
        pair = residual(DOWN0, 0, 2 * z) + residual(DOWN0, 0, 2 * z + 1)
        value = paired(pair, 1)
        ref[B, 1][z] = value
        ref[X, 1][z] = ref[SCALE, 1][z] * value

    send_level(DOWN1, 1)
    residual_inside(1)
    spread_to_peers(OWN_COEF, ALL_COEF, COEF_SEM, steps_away(5))
    face_weights()
    for level, planes in ((2, 8), (3, 4)):
        for z in (0, planes + 1):
            ref[WIDE_X, level][z] = jnp.zeros(WIDE, jnp.float32)
    receive(DOWN1)
    left = [residual(DOWN1, 1, z) for z in range(4)]
    pack_own_b([paired(left[2 * z] + left[2 * z + 1], 2) for z in range(2)])
    for z in range(4):
        ref[MID][z] = ref[X, 1][z] + ref[SCALE, 1][z] * left[z]

    spread_to_peers(OWN_B, ALL_B, B_SEM, [i for n in (5, 4, 3, 2, 1) for i in steps_away(n)])
    send_fields(MIDDLE, lambda dim, up: [ref[MID]], 4, 2)
    receive_from_peers(COEF_SEM)
    wide_coefs(2)
    wide_coefs(3)
    receive(RIMS0)
    receive(EDGES)
    receive(MIDDLE)
    receive_from_peers(B_SEM)
    wide_solve()

    rims = level_one()
    for z in range(NZ):
        ref[X, 0][z] = ref[X, 0][z] + ref[X, 1][z // 2]
    residual_inside(0)
    for z in range(NZ):
        acc = residual(DOWN0, 0, z)
        if z == 0:
            acc = acc - halo_z(RIMS0, 1, 0) * rims[0, 1]
        if z == NZ - 1:
            acc = acc - halo_z(RIMS0, 0, 0) * rims[0, 0]
        acc = acc - at_low(1, halo_y(RIMS0, 1, 0, z) * rims[1, 1][z // 2], 1)
        acc = acc - at_high(1, halo_y(RIMS0, 0, 0, z) * rims[1, 0][z // 2], 1)
        acc = acc - at_low(2, halo_x(RIMS0, 1, 0, z, 1) * rims[2, 1][z // 2], 1)
        acc = acc - at_high(2, halo_x(RIMS0, 0, 0, z, 1) * rims[2, 0][z // 2], 1)
        ref[R, 0][z] = acc
    for z in range(NZ):
        ref[X, 0][z] = ref[X, 0][z] + ref[SCALE, 0][z] * ref[R, 0][z]

    loads[WEIGHTS].wait()
    name = LAST
    stores = [pltpu.make_async_copy(adjoint_ref, adjoint_out, ref[OUT_SEM].at[3])]
    for dim in range(3):
        stores.append(
            pltpu.make_async_copy(gradient_ref.at[dim], gradient_out.at[dim], ref[OUT_SEM].at[dim])
        )
    for z in range(NZ):
        mask = ref[LOADED, ACTIVE][z].astype(jnp.float32)
        for c in range(3):
            adjoint_ref[c, z] = mask * (iterate[c, z] + ref[LOADED, WEIGHTS][c, z] * ref[X, 0][z])
    for c in range(3):
        ref[SEND, name, 0, 1][c] = adjoint_ref[c, NZ - 1]
        ref[SEND, name, 0, 0][c] = adjoint_ref[c, 0]
    send(name, 0)
    for z in range(NZ):
        for c in range(3):
            ref[SEND, name, 1, 1][c, z : z + 1, :] = adjoint_ref[c, z, NY - 1 : NY, :]
            ref[SEND, name, 1, 0][c, z : z + 1, :] = adjoint_ref[c, z, 0:1, :]
    send(name, 1)
    high, low = zero, zero
    for z in range(NZ):
        for c in range(3):
            high = packed(high, adjoint_ref[c, z], 1, c, z, 1)
            low = packed(low, adjoint_ref[c, z], 0, c, z, 1)
    ref[SEND, name, 2, 1][...] = high
    ref[SEND, name, 2, 0][...] = low
    send(name, 2)

    stores[0].start()
    face = ref[FACE]
    for dim in range(3):
        previous = None
        for z in range(NZ):
            flux = None
            for c in range(3):
                value = adjoint_ref[c, z]
                if dim == 0:
                    drop = value - adjoint_ref[c, z + 1] if z < NZ - 1 else value
                else:
                    drop = value - from_high(dim, value, 1)
                term = face[dim, c, z] * drop
                flux = term if flux is None else flux + term
            if dim == 0:
                gradient_ref[dim, z] = flux if previous is None else flux + previous
                previous = flux
            else:
                gradient_ref[dim, z] = flux + from_low(dim, flux, 1)
    for copy in copies[:-6]:
        copy.wait_send()
    receive(name)
    low_z, high_z = zero, zero
    for c in range(3):
        low_z = low_z + ref[FACE_LOW, 0][c] * (halo_z(name, 1, c) - adjoint_ref[c, 0])
        high_z = high_z + face[0, c, NZ - 1] * halo_z(name, 0, c)
    gradient_ref[0, 0] = gradient_ref[0, 0] + low_z
    gradient_ref[0, NZ - 1] = gradient_ref[0, NZ - 1] - high_z
    stores[1].start()
    for dim, halo in ((1, lambda *at: halo_y(name, *at)), (2, lambda *at: halo_x(name, *at, 1))):
        for z in range(NZ):
            low, high = zero, zero
            for c in range(3):
                rim = ref[FACE_LOW, 1][c, z : z + 1, :] if dim == 1 else ref[FACE_LOW, 2][c, z]
                low = low + rim * (halo(1, c, z) - adjoint_ref[c, z])
                high = high + face[dim, c, z] * halo(0, c, z)
            gradient_ref[dim, z] = gradient_ref[dim, z] + at_low(dim, low, 1) - at_high(dim, high, 1)
        stores[1 + dim].start()
    for store in stores:
        store.wait()
    for copy in copies[-6:]:
        copy.wait_send()


def hand_over(adjoint_in, gradient_in, adjoint_out, gradient_out, sems):
    arrays = ((adjoint_in, adjoint_out), (gradient_in, gradient_out))
    stores = [
        pltpu.make_async_copy(arrays[i][0].at[c], arrays[i][1].at[c], sems.at[3 * i + c])
        for i in range(2)
        for c in range(3)
    ]
    for store in stores:
        store.start()
    for store in stores:
        store.wait()


def solution(mesh):
    sizes = [mesh.shape[axis] for axis in AXES]

    def local(*args):
        table = scratch_table([(arg.shape, arg.dtype) for arg in args])
        out = jax.ShapeDtypeStruct((3, NZ) + PLANE, jnp.float32)
        results = pl.pallas_call(
            functools.partial(kernel, sizes, tuple(table)),
            out_shape=(out, out),
            in_specs=[pl.BlockSpec(memory_space=pl.ANY)] * len(args),
            out_specs=(pl.BlockSpec(memory_space=pl.ANY),) * 2,
            scratch_shapes=list(table.values()),
            compiler_params=pltpu.CompilerParams(collective_id=0, has_side_effects=True, vmem_limit_bytes=40 << 20),
        )(*[pltpu.with_memory_space_constraint(arg, pltpu.MemorySpace.HBM) for arg in args])
        return pl.pallas_call(
            hand_over,
            out_shape=(out, out),
            in_specs=[pl.BlockSpec(memory_space=pl.ANY)] * 2,
            out_specs=(pl.BlockSpec(memory_space=pl.ANY),) * 2,
            scratch_shapes=[pltpu.SemaphoreType.DMA((6,))],
            compiler_params=pltpu.CompilerParams(vmem_limit_bytes=40 << 20),
        )(*results)

    field = P("layer", "gy", "gx")
    stacked = P(None, "layer", "gy", "gx")
    return jax.shard_map(
        local,
        mesh=mesh,
        in_specs=(stacked, field) + (stacked,) * 8 + (field, stacked),
        out_specs=(stacked, stacked),
        check_vma=False,
    )
```
